512 devices in a mesh: req: 128 (over z, y, core), head: 4 (over x).
Axes of the slice: x: 4, y: 8, z: 8, core: 2. Of those that a mesh axis runs over, the one named last changes fastest.
Arguments:
- hidden_in: bfloat16 [256, 2048], P(None, 'head'), may hold values from -1.5 to 1.5
- attention_gain: float32 [2048], replicated, may hold values from 0.1 to 1.9
- query_gain: float32 [64], replicated, may hold values from 0.5 to 2
- key_gain: float32 [64], replicated, may hold values from 1.5 to 4
- feedforward_gain: float32 [2048], replicated, may hold values from 0.1 to 1.9
- input_weight: bfloat16 [2048, 1920], P('req', 'head'), may hold values from -0.125 to 0.125
- output_weight: bfloat16 [1280, 2048], P('req', 'head'), may hold values from -0.15625 to 0.15625
- gate_weight: bfloat16 [2048, 5120], P('req', 'head'), may hold values from -0.125 to 0.125
- up_weight: bfloat16 [2048, 5120], P('req', 'head'), may hold values from -0.125 to 0.125
- down_weight: bfloat16 [5120, 2048], P('req', 'head'), may hold values from -0.078125 to 0.078125
- old_cache: bfloat16 [4096, 128, 640], P(('req', 'head')), may hold values from -400 to 400
- keep_rows: int32 [4096, 64], P(('req', 'head')), may hold values from -1 to 127, as said below
- drop_weights: float32 [4096, 128], P(('req', 'head')), may hold values from 0.1 to 1
- dest_slots: int32 [512, 8], P(('req', 'head')), may hold values from 0 to 7, each once within a row
- lengths: int32 [256], replicated, may hold values from 1 to 16, 2048 in all
- page_table: int32 [256, 16], P('req'), may hold values from 0 to 7, as said below
- source: int32 [128], replicated, may hold values from 0 to 127, each once
Outputs:
- compact_cache: bfloat16 [2048, 128, 640], P(('req', 'head'))
- summary_rows: bfloat16 [4096, 640], P(('req', 'head'))
- hidden_out: bfloat16 [256, 2048], P(None, 'head')
The draws below stay inside these ranges and needn't reach their ends.
Inputs may be any that keep to these rules, and one draw needn't show every extreme that they name: `keep_rows`: row p lists kept rows of page p in ascending order, from 32 to 64 of them, then -1 to the end; some page keeps 64. `page_table`: row g * 2 + k belongs to the k-th request held by index g of req; entry j is the slot, on the device with req index g and head index j % 4, of that request's j-th page. On every device the entries that point to it form a permutation of its 8 slots. `source`: A permutation of the continued requests over the held slots. `dest_slots`: each row is a permutation. `lengths`: they sum to 2048 and the largest is 16.
All inputs are finite; a program needn't handle non-finite values.
Results may differ from the reference program's by a relative error of at most 0.015.
The reference program's roundings to bfloat16 on the way count: a program that leaves them out, or rounds other values in their place, can miss the bound.
Values may be sent and summed in bfloat16 or wider, within the bound.
A program may use at most 64 MiB of HBM per device.

```python
import math
import jax
import jax.numpy as jnp
import numpy as np
from jax import lax

D = 2048
HEADS = 20
KVH = 5
HD = 64
FF = 5120
PAGE = 128
KEEP = 64
NP = 16
R_DEV = 2
REQS = 256
CONT = 128
PG_DEV = 8
PAGES = 4096
KVW = 640
QKVW = 1920
N_REQ = 128
N_HEAD = 4


def draw_old_cache(key, part):
    first = jax.random.fold_in(key, 0)
    values = jnp.clip(jax.random.normal(first, (PAGES, PAGE, KVW), jnp.float32), -6.0, 6.0)
    return values.astype(jnp.bfloat16)


def draw_keep_rows(key, part):
    first, second, third = jax.random.split(key, 3)
    rows = jnp.arange(PAGE, dtype=jnp.int32)
    scores = jax.random.randint(first, (PAGES, PAGE), 0, 1 << 20, dtype=jnp.int32) * PAGE + rows[None, :]
    order = jnp.argsort(scores, axis=1).astype(jnp.int32)
    counts = jax.random.randint(second, (PAGES,), PAGE // 4, KEEP + 1, dtype=jnp.int32)
    forced = jax.random.randint(third, (PAGES,), 0, 4, dtype=jnp.int32) == 0
    counts = jnp.where(forced, KEEP, counts)
    chosen = order[:, :KEEP]
    slots = jnp.arange(KEEP, dtype=jnp.int32)
    marked = jnp.where(slots[None, :] < counts[:, None], chosen, 2 * PAGE)
    ordered = jnp.sort(marked, axis=1)
    return jnp.where(ordered >= PAGE, -1, ordered).astype(jnp.int32)


def draw_page_table(key, part):
    groups = REQS // R_DEV
    per_device = R_DEV * NP // N_HEAD
    device_keys = jax.random.split(key, groups * N_HEAD)
    shuffled = jax.vmap(lambda single: jax.random.permutation(single, per_device))(device_keys)
    table = shuffled.reshape(groups, N_HEAD, R_DEV, NP // N_HEAD)
    return jnp.transpose(table, (0, 2, 3, 1)).reshape(REQS, NP).astype(jnp.int32)


def shard_levels(rng, extent, shards, low, largest):
    def one(axis_at, shards_of):
        heights = jax.random.uniform(jax.random.fold_in(jax.random.fold_in(rng, 6), axis_at), (shards_of,), jnp.float32, low / len(shards), largest / len(shards))
        return jnp.repeat(jnp.exp(heights), extent[axis_at] // shards_of).reshape((-1,) + (1,) * (len(extent) - axis_at - 1))

    level = one(*shards[0])
    for cut in shards[1:]:
        level = level * one(*cut)
    return level


def length_profile(number_of, total, bound, slope):
    loads = [(1 << 20) // math.isqrt(standing ** slope) + 1 for standing in range(2, number_of + 1)]
    spare, given = total - bound - (number_of - 1), [1] * (number_of - 1)
    while spare > 0:
        free = [i for i in range(number_of - 1) if given[i] < bound]
        whole, left = sum([loads[i] for i in free]), spare
        for i in free:
            more = min(bound - given[i], max(1, left * loads[i] // whole), spare)
            given[i] = given[i] + more
            spare = spare - more
    return np.array([bound] + given)


def uneven(stream_key, amount, total, limit, skew):
    if amount == 2:
        one = jax.random.randint(stream_key, (), max(1, total - limit), min(limit, total - 1) + 1)
        return jnp.stack([one, total - one])
    tallies = jnp.asarray(length_profile(amount, total, limit, skew), jnp.int32)
    couples = (amount - 1) // 2
    donor, sink = tallies[1:1 + 2 * couples:2], tallies[2:2 + 2 * couples:2]
    slack = jnp.minimum(donor - 1, limit - sink)
    shifted = jax.random.randint(jax.random.fold_in(stream_key, 1), (couples,), 0, 1 << 20) % (slack + 1)
    tallies = tallies.at[1:1 + 2 * couples:2].set(donor - shifted).at[2:2 + 2 * couples:2].set(sink + shifted)
    return tallies[jax.random.permutation(jax.random.fold_in(stream_key, 2), amount)]


def normal_values(rng, dims, scale, reach, cuts=(), kind=jnp.bfloat16):
    values = jax.random.normal(rng, dims, jnp.float32) * scale
    if len(cuts) > 0:
        values = shard_levels(rng, dims, cuts, -0.22, 0.18) * values
    return jnp.clip(values, min=-reach, max=reach).astype(kind)


def setup_inputs(seed: int = 0) -> dict:
    key_list = jax.random.split(jax.random.key(seed), 18)
    return {
        "hidden_in": normal_values(key_list[0], (REQS, D), 0.1, 1.5, ((1, 4),)),
        "attention_gain": jnp.clip(1.0 + 0.18 * jax.random.normal(key_list[1], (D,), jnp.float32), 0.1, 1.9),
        "query_gain": jnp.clip(jax.random.uniform(key_list[2], (HD,), jnp.float32, 0.5, 2.0), 0.5, 2.0),
        "key_gain": jnp.clip(jax.random.uniform(key_list[3], (HD,), jnp.float32, 1.5, 4.0), 1.5, 4.0),
        "feedforward_gain": jnp.clip(1.0 + 0.18 * jax.random.normal(key_list[4], (D,), jnp.float32), 0.1, 1.9),
        "input_weight": normal_values(key_list[5], (D, QKVW), D ** -0.5, 0.125, ((0, 128), (1, 4))),
        "output_weight": normal_values(key_list[6], (HEADS * HD, D), (HEADS * HD) ** -0.5, 0.15625, ((0, 128), (1, 4))),
        "gate_weight": normal_values(key_list[7], (D, FF), D ** -0.5, 0.125, ((0, 128), (1, 4))),
        "up_weight": normal_values(key_list[8], (D, FF), D ** -0.5, 0.125, ((0, 128), (1, 4))),
        "down_weight": normal_values(key_list[9], (FF, D), FF ** -0.5, 0.078125, ((0, 128), (1, 4))),
        "old_cache": draw_old_cache(jax.random.fold_in(key_list[17], 71), 0),
        "keep_rows": draw_keep_rows(jax.random.fold_in(key_list[17], 71), 0),
        "drop_weights": jnp.clip(jnp.exp(math.log(1.0) - 2.3025851 * jax.random.uniform(key_list[12], (PAGES, PAGE), jnp.float32) ** shard_levels(key_list[12], (PAGES, PAGE), ((0, 512),), -0.2, 0.2)), 0.1, 1.0),
        "dest_slots": jax.vmap(lambda own: jax.random.permutation(own, PG_DEV))(jax.random.split(key_list[13], (N_REQ * N_HEAD))).reshape((N_REQ * N_HEAD, PG_DEV)).astype(jnp.int32),
        "lengths": uneven(key_list[14], REQS, REQS * NP // 2, NP, 1).astype(jnp.int32),
        "page_table": draw_page_table(jax.random.fold_in(key_list[17], 71), 0),
        "source": jax.random.permutation(key_list[16], CONT).astype(jnp.int32),
    }


epsilon = 1e-06
negative = -1e+30

def rms_rows(values, gain):
    mean_square = lax.optimization_barrier(jnp.mean(values * values, axis=-1, keepdims=True))
    return values * lax.rsqrt(mean_square + epsilon) * gain

def rotate(vectors, positions):
    half = vectors.shape[-1] // 2
    frequency = 10000.0 ** (-jnp.arange(half, dtype=jnp.float32) / half)
    angles = positions.astype(jnp.float32)[:, None] * frequency[None, :]
    cosine = jnp.cos(angles)[:, None, :]
    sine = jnp.sin(angles)[:, None, :]
    first = vectors[..., :half]
    second = vectors[..., half:]
    return jnp.concatenate([first * cosine - second * sine, second * cosine + first * sine], axis=-1)

def compact_block(block):
    pages, keep, weights = block
    rows = jnp.arange(pages.shape[1], dtype=jnp.int32)
    picks = (keep[:, :, None] == rows[None, None, :]).astype(jnp.float32)
    wide = pages.astype(jnp.float32)
    kept = jnp.einsum('pkr,prc->pkc', picks, wide, precision=lax.Precision.HIGHEST).astype(jnp.bfloat16)
    dropped = weights * (1.0 - lax.optimization_barrier(jnp.sum(picks, axis=1)))
    total = lax.optimization_barrier(jnp.sum(dropped, axis=1))
    means = jnp.einsum('pr,prc->pc', dropped, wide, precision=lax.Precision.HIGHEST) / total[:, None]
    return (kept, means.astype(jnp.bfloat16), jnp.log(total))

def reference(hidden_in, attention_gain, query_gain, key_gain, feedforward_gain, input_weight, output_weight, gate_weight, up_weight, down_weight, old_cache, keep_rows, drop_weights, dest_slots, lengths, page_table, source):
    devices = N_REQ * N_HEAD
    half = R_DEV // 2
    split = KVH * HD
    ratio = HEADS // KVH
    scale = HD ** (-0.5)
    blocks = (old_cache.reshape(devices, PG_DEV, PAGE, KVW), keep_rows.reshape(devices, PG_DEV, KEEP), drop_weights.reshape(devices, PG_DEV, PAGE))
    kept, means, bias = lax.map(compact_block, blocks)
    slot_ids = jnp.arange(PG_DEV, dtype=jnp.int32)
    inverse = lax.optimization_barrier(jnp.sum(jnp.where(dest_slots[:, None, :] == slot_ids[None, :, None], slot_ids[None, None, :], 0), axis=2)).astype(jnp.int32)
    fresh = jnp.take_along_axis(kept, inverse[:, :, None, None], axis=1)
    compact_cache = fresh.reshape(PAGES // 2, PAGE, KVW)
    summary_rows = jnp.take_along_axis(means, inverse[:, :, None], axis=1).reshape(PAGES, KVW)
    kept_flat = kept.reshape(PAGES, KEEP, KVW)
    means_flat = means.reshape(PAGES, KVW)
    bias_flat = bias.reshape(PAGES)
    normed = rms_rows(hidden_in.astype(jnp.float32), attention_gain).astype(jnp.bfloat16)
    qkv = jnp.dot(normed, input_weight, preferred_element_type=jnp.float32).astype(jnp.bfloat16)
    qkv = lax.optimization_barrier(qkv).astype(jnp.float32)
    positions = lengths * PAGE
    query = rotate(rms_rows(qkv[:, :HEADS * HD].reshape(REQS, HEADS, HD), query_gain), positions).astype(jnp.bfloat16)
    key_new = rotate(rms_rows(qkv[:, HEADS * HD:(HEADS + KVH) * HD].reshape(REQS, KVH, HD), key_gain), positions).astype(jnp.bfloat16)
    value_new = qkv[:, (HEADS + KVH) * HD:].reshape(REQS, KVH, HD)
    rows_all = jnp.arange(REQS, dtype=jnp.int32)
    inverse_source = jnp.zeros((CONT,), jnp.int32).at[source].set(jnp.arange(CONT, dtype=jnp.int32))
    position = rows_all % R_DEV
    slot = rows_all // R_DEV * half + position - half
    owner = inverse_source[jnp.clip(slot, 0, CONT - 1)]
    held_to_req = jnp.where(position < half, rows_all, owner // half * R_DEV + half + owner % half).astype(jnp.int32)

    def attend(row):
        group = row // R_DEV
        request = held_to_req[row]
        logical = jnp.arange(NP, dtype=jnp.int32)
        ids = ((group * N_HEAD + logical % N_HEAD) * PG_DEV + page_table[row]).astype(jnp.int32)
        live = logical < lengths[request]
        entries = kept_flat[ids].astype(jnp.float32)
        row_live = (keep_rows[ids] >= 0) & live[:, None]
        summary = means_flat[ids].astype(jnp.float32)
        query_here = query[request].astype(jnp.float32).reshape(KVH, ratio, HD)
        key_here = key_new[request].astype(jnp.float32)
        value_here = value_new[request]
        row_keys = entries[:, :, :split].reshape(NP, KEEP, KVH, HD)
        row_values = entries[:, :, split:].reshape(NP, KEEP, KVH, HD)
        row_scores = jnp.einsum('ngd,jmnd->ngjm', query_here, row_keys, precision=lax.Precision.HIGHEST) * scale
        row_scores = jnp.where(row_live[None, None], row_scores, negative)
        mean_scores = jnp.einsum('ngd,jnd->ngj', query_here, summary[:, :split].reshape(NP, KVH, HD), precision=lax.Precision.HIGHEST) * scale + bias_flat[ids][None, None, :]
        mean_scores = jnp.where(live[None, None], mean_scores, negative)
        own_score = jnp.einsum('ngd,nd->ng', query_here, key_here, precision=lax.Precision.HIGHEST) * scale
        top = jnp.maximum(jnp.maximum(lax.optimization_barrier(jnp.max(row_scores, axis=(2, 3))), lax.optimization_barrier(jnp.max(mean_scores, axis=2))), own_score)
        row_weight = jnp.where(row_live[None, None], jnp.exp(row_scores - top[:, :, None, None]), 0.0)
        mean_weight = jnp.where(live[None, None], jnp.exp(mean_scores - top[:, :, None]), 0.0)
        own_weight = jnp.exp(own_score - top)
        mass = lax.optimization_barrier(jnp.sum(row_weight, axis=(2, 3))) + lax.optimization_barrier(jnp.sum(mean_weight, axis=2)) + own_weight
        total = jnp.einsum('ngjm,jmnd->ngd', row_weight, row_values, precision=lax.Precision.HIGHEST)
        total = total + jnp.einsum('ngj,jnd->ngd', mean_weight, summary[:, split:].reshape(NP, KVH, HD), precision=lax.Precision.HIGHEST)
        total = total + own_weight[:, :, None] * value_here[:, None, :]
        return (total / mass[:, :, None]).reshape(HEADS * HD).astype(jnp.bfloat16)
    attention_held = lax.map(attend, rows_all)
    attention = jnp.zeros((REQS, HEADS * HD), jnp.bfloat16).at[held_to_req].set(attention_held)
    projected = jnp.dot(attention, output_weight, preferred_element_type=jnp.float32)
    mid = (hidden_in.astype(jnp.float32) + projected).astype(jnp.bfloat16)
    mid = lax.optimization_barrier(mid).astype(jnp.float32)
    normed_mid = rms_rows(mid, feedforward_gain).astype(jnp.bfloat16)
    gate = jnp.dot(normed_mid, gate_weight, preferred_element_type=jnp.float32)
    upper = jnp.dot(normed_mid, up_weight, preferred_element_type=jnp.float32)
    active = (jax.nn.silu(gate) * upper).astype(jnp.bfloat16)
    hidden_out = (mid + jnp.dot(active, down_weight, preferred_element_type=jnp.float32)).astype(jnp.bfloat16)
    return (compact_cache, summary_rows, hidden_out)
```

```python
import jax
import jax.numpy as jnp
from jax import lax
from jax.experimental import pallas as pl
from jax.experimental.pallas import tpu as pltpu
from jax.sharding import PartitionSpec as P

D = 2048
HEADS = 20
KVH = 5
HD = 64
PAGE = 128
KEEP = 64
NP = 16
R_DEV = 2
KVW = 640
QROWS = 24

epsilon = 1e-06
negative = -1e30
bf16 = jnp.bfloat16
f32 = jnp.float32
i32 = jnp.int32


def iota(shape, dim):
    return lax.broadcasted_iota(i32, shape, dim)


def dot(a, b):
    return jnp.dot(a, b, preferred_element_type=f32)


def dot_t(a, b):
    return lax.dot_general(a, b, (((1,), (1,)), ((), ())), preferred_element_type=f32)


def rounded(values):
    return values.astype(bf16).astype(f32)


def at_lane(values, lane):
    return jnp.sum(jnp.where(iota(values.shape, 1) == lane, values, 0.0), axis=1, keepdims=True)


def kernel(
    hidden_ref, held_ref, win_ref, wo_ref, wg_ref, wu_ref, wd_ref,
    cache_ref, keep_ref, drop_ref, inv_ref, cos_ref, sin_ref, allow_ref,
    again_ref, fgain_ref, qgain_ref, kgain_ref,
    compact_ref, summary_ref, out_ref,
    hx, win_s, wo_s, gu_s, wd_s, win_w, wo_w, gu_w, wd_w,
    pb, rb, cx, fa, kv, tail, dx, eb, ex, xa, ox, mx, mid_f, gs, gx, ax, ys, yx, jx, sumr, means,
    s_w1, r_w1, s_z, r_z, s_ring, r_ring, s_ph, r_ph,
):
    group = lax.axis_index("req")
    x = lax.axis_index("head")
    z = group // 16
    yc = lax.rem(group, 16)
    ya = yc // 4
    yb = lax.rem(yc, 4)
    y = yc // 2
    c = lax.rem(yc, 2)
    col = x * 4 + ya

    def dev(zz, yy, xx):
        return {"req": zz * 16 + yy, "head": xx}

    def remote(src, dst, ssem, rsem, target):
        return pltpu.make_async_remote_copy(
            src_ref=src, dst_ref=dst, send_sem=ssem, recv_sem=rsem,
            device_id=target, device_id_type=pl.DeviceIdType.MESH,
        )

    def yc_peer(j):
        return lax.rem(yc + j, 16)

    def col_peer(j):
        return lax.rem(col + j, 16)

    def x_peer(j):
        return lax.rem(x + j, 4)

    def yb_peer(j):
        return lax.rem(yb + j, 4)

    def z_peer(j):
        return lax.rem(z + j, 8)

    wd_w[:, :, 6:8] = jnp.zeros((8, 2, 2, 16, 128), bf16)

    barrier = pltpu.get_barrier_semaphore()

    def greet(target):
        pl.semaphore_signal(barrier, inc=1, device_id=target, device_id_type=pl.DeviceIdType.MESH)

    @pl.loop(1, 16)
    def _(j):
        greet(dev(z, yc_peer(j), x))

    @pl.loop(0, 12)
    def _(j):
        greet(dev(z, (j // 3) * 4 + yb, x_peer(1 + lax.rem(j, 3))))

    @pl.loop(1, 8)
    def _(j):
        greet(dev(z_peer(j), yc, x))

    win = win_ref[...]
    pad = jnp.zeros((16, 32), bf16)
    even = jnp.concatenate([win, pad], axis=1)
    odd = jnp.concatenate([pad, win], axis=1)
    shifted = jnp.where(lax.rem(x, 2) == 0, even, odd)
    wo_s[...] = jnp.zeros_like(wo_s)
    wd_s[...] = jnp.zeros_like(wd_s)
    gu_s[...] = jnp.zeros_like(gu_s)
    wo_full = jnp.concatenate([wo_ref[...], jnp.zeros((6, 512), bf16)], axis=0)
    wd_full = jnp.concatenate([wd_ref[...], jnp.zeros((8, 512), bf16)], axis=0)
    gate = wg_ref[...]
    up = wu_ref[...]
    for a in range(4):
        lanes = slice(a * 128, (a + 1) * 128)
        win_s[a] = shifted[:, lanes]
        wo_s[a] = wo_full[:, lanes]
        for k in range(3):
            wd_s[a, k] = wd_full[k * 16:(k + 1) * 16, lanes]
        for k in range(4):
            for h in range(2):
                first = a * 320 + k * 80 + h * 40
                gu_s[a, :, k * 256 + h * 48:k * 256 + h * 48 + 40] = gate[:, first:first + 40]
                gu_s[a, :, k * 256 + 128 + h * 48:k * 256 + 128 + h * 48 + 40] = up[:, first:first + 40]

    chosen = (held_ref[...] == iota((32, 256), 1)).astype(bf16)
    rows_here = dot(chosen, hidden_ref[...]).astype(bf16)
    hx[x] = rows_here

    pl.semaphore_wait(barrier, 34)

    def h_copy(j):
        return remote(hx.at[x], hx.at[x], s_ph.at[0], r_ph.at[0], dev(z, yc, x_peer(j)))

    cls = lax.rem(y, 4)
    yh = y // 4
    slot = yh * 2 + c

    def w1_parts(a):
        return (
            (win_s.at[a], win_w.at[z, slot], 0),
            (wo_s.at[a], wo_w.at[z, slot], 1),
            (gu_s.at[a], gu_w.at[z, slot], 2),
            (wd_s.at[a], wd_w.at[z, yh, pl.ds(c * 3, 3)], 3),
        )

    for m in range(4):
        for a in range(4):
            src, dst, which = w1_parts(a)[m]
            target = a * 4 + cls

            @pl.when(target != yc)
            def _():
                remote(src, dst, s_w1.at[which, a], r_w1.at[which], dev(z, target, x)).start()

            @pl.when(target == yc)
            def _():
                pltpu.make_async_copy(src, dst, r_w1.at[which]).start()

        if m == 0:
            for j in range(1, 4):
                h_copy(j).start()

    def w1_wait(which, block):
        pltpu.make_async_copy(block, block, r_w1.at[which]).wait()

    def z_copy(which, buf, j):
        return remote(buf.at[z], buf.at[z], s_z.at[which], r_z.at[which], dev(z_peer(j), yc, x))

    def seven(buf):
        return buf.at[pl.ds(0, 7)]

    w1_wait(0, win_w.at[z])

    @pl.loop(1, 8)
    def _(j):
        z_copy(0, win_w, j).start()

    w1_wait(1, wo_w.at[z])

    @pl.loop(1, 8)
    def _(j):
        z_copy(1, wo_w, j).start()

    w1_wait(2, gu_w.at[z])
    w1_wait(3, wd_w.at[z, :, pl.ds(0, 6)])

    def ring(step, way, which):
        block = lax.rem(z - (step - 1) + 8, 8) if way == 0 else lax.rem(z + step - 1, 8)
        target = lax.rem(z + 1, 8) if way == 0 else lax.rem(z + 7, 8)
        ref = gu_w.at[block] if which == 0 else wd_w.at[block, :, pl.ds(0, 6)]
        return remote(ref, ref, s_ring.at[way, step - 1, which], r_ring.at[way, step - 1, which], dev(target, yc, x))

    def ways(step):
        return (0, 1) if step < 4 else (0,)

    def ring_step(step):
        for which in range(2):
            for way in (0, 1):
                if step > 1 and way in ways(step - 1):
                    ring(step - 1, way, which).wait_recv()
            if step <= 4:
                for way in ways(step):
                    ring(step, way, which).start()

    ring_step(1)

    bias = jnp.zeros((1, 640), f32)
    tail[...] = jnp.zeros_like(tail)
    lane640 = iota((1, 640), 1)
    row_ids = iota((64, 128), 1)
    keep_all = keep_ref[...]
    for p in range(8):
        picks = (keep_all[:, p:p + 1] == row_ids).astype(f32)
        weight = drop_ref[p:p + 1, :] * (1.0 - jnp.sum(picks, axis=0, keepdims=True))
        total = jnp.sum(weight, axis=1, keepdims=True)
        w1 = rounded(weight)
        w2 = rounded(weight - w1)
        w3 = weight - w1 - w2
        left = jnp.concatenate([picks, w1, w2, w3, jnp.zeros((13, 128), f32)], axis=0).astype(bf16)
        got = dot(left, cache_ref[p])
        kv[p] = got[0:64].astype(bf16)
        mean = rounded((got[64:65] + got[65:66] + got[66:67]) / total)
        tail[p:p + 1, :] = mean
        means[p] = mean
        bias = jnp.where(lane640 == 512 + p, jnp.log(total), bias)

    for f in range(8):
        page = inv_ref[f]
        compact_ref[f // 2, (f % 2) * 64:(f % 2) * 64 + 64, :] = kv[page]
        sumr[f:f + 1, :] = means[page]
    summary_ref[...] = sumr[...].astype(bf16)

    sel_row = iota((512, 128), 0)
    sel_col = iota((512, 128), 1)
    select = (
        ((sel_row & 127) >> 5 == yb)
        & (sel_col >> 5 == sel_row >> 7)
        & ((sel_row & 31) == (sel_col & 31))
    ).astype(bf16)

    pltpu.make_async_copy(hx.at[pl.ds(0, 3)], hx.at[pl.ds(0, 3)], r_ph.at[0]).wait()
    square = jnp.zeros((32, 1), f32)
    for k in range(4):
        part = hx[k].astype(f32)
        square += jnp.sum(part * part, axis=1, keepdims=True)
    scale = lax.rsqrt(square * (1.0 / D) + epsilon)
    pieces = []
    for k in range(4):
        normed = (hx[k].astype(f32) * scale * again_ref[:, k * 512:(k + 1) * 512]).astype(bf16)
        pieces.append(dot(normed, select).astype(bf16))
    x_in = jnp.concatenate(pieces, axis=1)

    pltpu.make_async_copy(seven(win_w), seven(win_w), r_z.at[0]).wait()
    partial = dot(x_in, win_w[...].reshape(512, 128))
    for k in range(16):
        pb[k] = partial[2 * k:2 * k + 2, :]
    rb[yc] = pb[yc]

    def b_copy(j):
        return remote(pb.at[yc_peer(j)], rb.at[yc], s_ph.at[1], r_ph.at[1], dev(z, yc_peer(j), x))

    @pl.loop(1, 16)
    def _(j):
        b_copy(j).start()

    ring_step(2)
    fifteen = pl.ds(0, 15)
    pltpu.make_async_copy(rb.at[fifteen], rb.at[fifteen], r_ph.at[1]).wait()
    for a in range(4):
        cx[x, a] = rounded(rb[4 * a] + rb[4 * a + 1] + rb[4 * a + 2] + rb[4 * a + 3])

    def c_copy(j):
        return remote(cx.at[x], cx.at[x], s_ph.at[2], r_ph.at[2], dev(z, yc, x_peer(j)))

    for j in range(1, 4):
        c_copy(j).start()
    three = pl.ds(0, 3)
    pltpu.make_async_copy(cx.at[three], cx.at[three], r_ph.at[2]).wait()
    for k in range(16):
        fa[2 * k:2 * k + 2, :] = cx[k // 4, k % 4]

    mixed = fa[...]
    row = iota((32, 128), 0)
    lane = iota((32, 128), 1)
    low = lane < 64
    block = row >> 1
    moved = pltpu.roll(pltpu.roll(mixed, 30, 0), 64, 1)
    mixed = jnp.where(((block == 3) | (block == 11)) & ~low, mixed + moved, mixed)
    sq = mixed * mixed
    ms_low = jnp.sum(jnp.where(low, sq, 0.0), axis=1, keepdims=True) * (1.0 / HD)
    ms_high = jnp.sum(jnp.where(low, 0.0, sq), axis=1, keepdims=True) * (1.0 / HD)
    inverse = jnp.where(low, lax.rsqrt(ms_low + epsilon), lax.rsqrt(ms_high + epsilon))
    place = block * 2 + jnp.where(low, 0, 1)
    gain = jnp.where(place <= 20, qgain_ref[...], kgain_ref[...])
    vec = mixed * inverse * gain
    even_row = (row & 1) == 0
    cosine = jnp.where(even_row, cos_ref[0:1, :], cos_ref[1:2, :])
    sine = jnp.where(even_row, sin_ref[0:1, :], sin_ref[1:2, :])
    first_half = (lane & 63) < 32
    rotated = jnp.where(
        first_half,
        vec * cosine - pltpu.roll(vec, 96, 1) * sine,
        vec * cosine + pltpu.roll(vec, 32, 1) * sine,
    )
    final = jnp.where(place >= 27, mixed, rounded(rotated))
    swapped = pltpu.roll(final, 64, 1)
    low2 = low[0:2]

    def two(values, b):
        return values[2 * b:2 * b + 2, :]

    tail[8:10, 0:128] = jnp.where(low2, two(swapped, 10), two(swapped, 11))
    tail[8:10, 128:256] = jnp.where(low2, two(swapped, 11), two(final, 12))
    tail[8:10, 256:384] = two(final, 13)
    tail[8:10, 384:512] = two(final, 14)
    tail[8:10, 512:640] = two(final, 15)
    kv[8, 0:16] = tail[...].astype(bf16)
    kv[8, 16:64] = jnp.zeros((48, 640), bf16)
    kv[9] = jnp.zeros((64, 640), bf16)

    lowq = low[0:QROWS]
    fq = final[0:QROWS]
    gq = swapped[0:QROWS]
    both = jnp.concatenate([jnp.where(lowq, fq, gq), jnp.where(lowq, gq, fq)], axis=0)
    nrow = 2 * QROWS

    def row_facts(width):
        at = iota((nrow, width), 0)
        second = at >= QROWS
        inside = jnp.where(second, at - QROWS, at)
        request = inside & 1
        spot = (inside >> 1) * 2 + jnp.where(second, 1, 0)
        head = jnp.where(spot <= 7, spot, spot - 1)
        valid = (spot != 8) & (spot <= 20)
        return request, head, valid

    request, head, valid = row_facts(384)
    lane384 = iota((nrow, 384), 1)
    queries = jnp.where(
        valid & (lane384 >> 6 == head >> 2), jnp.concatenate([both, both, both], axis=1), 0.0
    ).astype(bf16)
    scores = dot_t(queries, kv[:, :, 0:384].reshape(640, 384)) * (HD ** (-0.5)) + bias
    request640, _, _ = row_facts(640)
    permit = jnp.where(request640 == 0, allow_ref[0:1, :], allow_ref[1:2, :]) > 0.5
    scores = jnp.where(permit, scores, negative)
    top = jnp.max(scores, axis=1, keepdims=True)
    weight = jnp.where(permit, jnp.exp(scores - top), 0.0)
    mass = jnp.sum(weight, axis=1, keepdims=True)
    w1 = rounded(weight)
    w2 = rounded(weight - w1)
    w3 = weight - w1 - w2
    summed = dot(jnp.concatenate([w1, w2, w3], axis=0).astype(bf16), kv[:, :, 256:640].reshape(640, 384))
    summed = summed[0:nrow] + summed[nrow:2 * nrow] + summed[2 * nrow:3 * nrow]
    summed = jnp.where(lane384 >> 6 == (head >> 2) + 1, summed, 0.0)
    folded = summed[:, 0:128] + summed[:, 128:256] + summed[:, 256:384]
    folded = folded + pltpu.roll(folded, 64, 1)
    lane128 = iota((nrow, 128), 1)
    dx[x] = jnp.where(
        lane128 < 64, folded, jnp.where(lane128 == 64, mass, jnp.where(lane128 == 65, top, 0.0))
    )

    def d_copy(j):
        return remote(dx.at[x], dx.at[x], s_ph.at[3], r_ph.at[3], dev(z, yc, x_peer(j)))

    for j in range(1, 4):
        d_copy(j).start()
    ring_step(3)

    kap = iota((1, 2048), 1)
    kclass = kap >> 9
    kz = (kap >> 6) & 7
    kyh = (kap >> 5) & 1
    kc = (kap >> 4) & 1
    ki = kap & 15
    feature = 10 * (kz * 16 + (4 * kyh + kclass) * 2 + kc) + ki
    real = ki < 10
    spread = (((feature & 63) == iota((128, 2048), 0)) & real).astype(bf16)

    pltpu.make_async_copy(dx.at[three], dx.at[three], r_ph.at[3]).wait()
    parts = [dx[k] for k in range(4)]
    tops = [at_lane(part, 65) for part in parts]
    best = jnp.maximum(jnp.maximum(tops[0], tops[1]), jnp.maximum(tops[2], tops[3]))
    acc = jnp.zeros((nrow, 128), f32)
    for k in range(4):
        acc += parts[k] * jnp.exp(tops[k] - best)
    attention = jnp.where(lane128 < 64, acc / at_lane(acc, 64), 0.0).astype(bf16)
    _, head2048, valid2048 = row_facts(2048)
    spread_rows = dot(attention, spread)
    spread_rows = jnp.where(valid2048 & (head2048 == feature >> 6), spread_rows, 0.0).astype(bf16)
    pick_at = iota((8, nrow), 1)
    pick_second = jnp.where(pick_at >= QROWS, pick_at - QROWS, pick_at)
    pick = ((pick_second & 1) == iota((8, nrow), 0)).astype(bf16)
    grouped = dot(pick, spread_rows)
    for k in range(4):
        eb[k] = grouped[0:2, k * 512:(k + 1) * 512]
    ex[yc] = eb[yb]

    def e_copy(j):
        return remote(
            eb.at[lax.rem(yc_peer(j), 4)], ex.at[yc], s_ph.at[4], r_ph.at[4], dev(z, yc_peer(j), x)
        )

    @pl.loop(1, 16)
    def _(j):
        e_copy(j).start()

    ring_step(4)
    pltpu.make_async_copy(seven(wo_w), seven(wo_w), r_z.at[1]).wait()
    pltpu.make_async_copy(ex.at[fifteen], ex.at[fifteen], r_ph.at[4]).wait()
    for k in range(16):
        xa[2 * k:2 * k + 2, :] = ex[k]
    ox[yb] = dot(xa[...].astype(bf16), wo_w[...].reshape(512, 128))

    def o_copy(j):
        return remote(ox.at[yb], ox.at[yb], s_ph.at[5], r_ph.at[5], dev(z, ya * 4 + yb_peer(j), x))

    for j in range(1, 4):
        o_copy(j).start()
    pltpu.make_async_copy(ox.at[three], ox.at[three], r_ph.at[5]).wait()
    residual = jnp.zeros((32, 128), f32)
    own_rows = hx[x]
    for k in range(4):
        residual = jnp.where(ya == k, own_rows[:, k * 128:(k + 1) * 128].astype(f32), residual)
    mid = (residual + (ox[0] + ox[1] + ox[2] + ox[3])).astype(bf16)
    mx[col] = mid
    mid_f[...] = mid.astype(f32)

    def m_copy(buf, n, j):
        peer = col_peer(j)
        return remote(
            buf.at[col], buf.at[col], s_ph.at[n], r_ph.at[n], dev(z, lax.rem(peer, 4) * 4 + yb, peer // 4)
        )

    @pl.loop(1, 16)
    def _(j):
        m_copy(mx, 6, j).start()

    pltpu.make_async_copy(mx.at[fifteen], mx.at[fifteen], r_ph.at[6]).wait()
    square = jnp.zeros((32, 128), f32)
    for k in range(16):
        part = mx[k].astype(f32)
        square += part * part
    scale = lax.rsqrt(jnp.sum(square, axis=1, keepdims=True) * (1.0 / D) + epsilon)
    pieces = []
    for u in range(4):
        tiles = []
        for t in range(4):
            k = 4 * u + t
            tiles.append((mx[k].astype(f32) * scale * fgain_ref[:, k * 128:(k + 1) * 128]).astype(bf16))
        pieces.append(dot(jnp.concatenate(tiles, axis=1), select).astype(bf16))
    x_mid = jnp.concatenate(pieces, axis=1)

    ring_step(5)
    for k in range(4):
        gs[k] = dot(x_mid, gu_w[:, :, :, k * 256:(k + 1) * 256].reshape(512, 256))
    gx[yb] = gs[yb]

    def g_copy(j):
        return remote(gs.at[yb_peer(j)], gx.at[yb], s_ph.at[7], r_ph.at[7], dev(z, ya * 4 + yb_peer(j), x))

    for j in range(1, 4):
        g_copy(j).start()
    pltpu.make_async_copy(gx.at[three], gx.at[three], r_ph.at[7]).wait()
    sums = gx[0] + gx[1] + gx[2] + gx[3]
    gate_sum = sums[:, 0:128]
    ax[col] = (gate_sum / (1.0 + jnp.exp(-gate_sum)) * sums[:, 128:256]).astype(bf16)

    @pl.loop(1, 16)
    def _(j):
        m_copy(ax, 8, j).start()

    pltpu.make_async_copy(ax.at[fifteen], ax.at[fifteen], r_ph.at[8]).wait()
    whole = jnp.concatenate([ax[k] for k in range(16)], axis=1)
    down = dot(whole, wd_w[...].reshape(2048, 128))
    for k in range(4):
        ys[k] = down[8 * k:8 * k + 8, :]
    yx[yb] = ys[yb]

    def y_copy(j):
        return remote(ys.at[yb_peer(j)], yx.at[yb], s_ph.at[9], r_ph.at[9], dev(z, ya * 4 + yb_peer(j), x))

    for j in range(1, 4):
        y_copy(j).start()
    pltpu.make_async_copy(yx.at[three], yx.at[three], r_ph.at[9]).wait()
    mine = mid_f[pl.ds(pl.multiple_of(yb * 8, 8), 8), :]
    jx[c, y, z] = (mine + (yx[0] + yx[1] + yx[2] + yx[3])).astype(bf16)

    def jz_copy(j):
        return remote(jx.at[c, y, z], jx.at[c, y, z], s_ph.at[10], r_ph.at[10], dev(z_peer(j), yc, x))

    @pl.loop(1, 8)
    def _(j):
        jz_copy(j).start()

    pltpu.make_async_copy(jx.at[0, 0, pl.ds(0, 7)], jx.at[0, 0, pl.ds(0, 7)], r_ph.at[10]).wait()

    def jy_copy(j):
        return remote(
            jx.at[c, y], jx.at[c, y], s_ph.at[11], r_ph.at[11], dev(z, lax.rem(y + j, 8) * 2 + c, x)
        )

    @pl.loop(1, 8)
    def _(j):
        jy_copy(j).start()

    pltpu.make_async_copy(jx.at[0, pl.ds(0, 7)], jx.at[0, pl.ds(0, 7)], r_ph.at[11]).wait()
    last = remote(jx.at[c], jx.at[c], s_ph.at[12], r_ph.at[12], dev(z, y * 2 + 1 - c, x))
    last.start()
    last.wait_recv()
    out_ref[...] = jx[...]

    last.wait_send()

    def sent(block, sem):
        pltpu.make_async_copy(block, block, sem).wait()

    for m in range(4):
        for a in range(4):
            src, dst, which = w1_parts(a)[m]
            target = a * 4 + cls

            @pl.when(target != yc)
            def _():
                remote(src, dst, s_w1.at[which, a], r_w1.at[which], dev(z, target, x)).wait_send()

    sent(seven(win_w), s_z.at[0])
    sent(seven(wo_w), s_z.at[1])
    for step in range(1, 5):
        for which in range(2):
            for way in ways(step):
                ring(step, way, which).wait_send()
    sent(hx.at[three], s_ph.at[0])
    sent(rb.at[fifteen], s_ph.at[1])
    sent(cx.at[three], s_ph.at[2])
    sent(dx.at[three], s_ph.at[3])
    sent(ex.at[fifteen], s_ph.at[4])
    sent(ox.at[three], s_ph.at[5])
    sent(mx.at[fifteen], s_ph.at[6])
    sent(gx.at[three], s_ph.at[7])
    sent(ax.at[fifteen], s_ph.at[8])
    sent(yx.at[three], s_ph.at[9])
    sent(jx.at[0, 0, pl.ds(0, 7)], s_ph.at[10])
    sent(jx.at[0, pl.ds(0, 7)], s_ph.at[11])


def held_request(rows, source):
    half = R_DEV // 2
    position = rows % R_DEV
    slot = rows // R_DEV * half + position - half
    continued = jnp.arange(source.shape[0], dtype=i32)
    matches = source[None, :] == slot[:, None]
    owner_cont = jnp.sum(jnp.where(matches, continued[None, :], 0), axis=1)
    carried = owner_cont // half * R_DEV + half + owner_cont % half
    return jnp.where(position < half, rows, carried)


def on_device(
    hidden_in, attention_gain, query_gain, key_gain, feedforward_gain,
    input_weight, output_weight, gate_weight, up_weight, down_weight,
    old_cache, keep_rows, drop_weights, dest_slots, lengths, page_table, source,
):
    lanes = lax.axis_size("head")
    group = lax.axis_index("req")
    lane = lax.axis_index("head")
    z = group // 16
    team = held_request(z * 32 + jnp.arange(32, dtype=i32), source)
    held = held_request(group * R_DEV + jnp.arange(R_DEV, dtype=i32), source)
    held_len = lengths[held]
    half = HD // 2
    frequency = 10000.0 ** (-jnp.arange(half, dtype=f32) / half)
    angles = (held_len * PAGE).astype(f32)[:, None] * frequency[None, :]
    cosine = jnp.tile(jnp.cos(angles), (1, 4))
    sine = jnp.tile(jnp.sin(angles), (1, 4))
    fresh_ids = jnp.arange(8, dtype=i32)
    inverse = jnp.sum(
        jnp.where(dest_slots[0][None, :] == fresh_ids[:, None], fresh_ids[None, :], 0), axis=1
    )
    per_lane = NP // lanes
    table = page_table.reshape(R_DEV, per_lane, lanes)
    mine = lax.dynamic_slice_in_dim(table, lane, 1, 2)[:, :, 0]
    logical = jnp.arange(per_lane, dtype=i32) * lanes + lane
    live = logical[None, :] < held_len[:, None]
    owner = jnp.any((mine[:, :, None] == fresh_ids[None, None, :]) & live[:, :, None], axis=1)
    row_live = keep_rows >= 0
    allow_rows = (owner[:, :, None] & row_live[None]).reshape(R_DEV, 512)
    own = (jnp.arange(R_DEV)[:, None] == jnp.arange(120)[None, :]) & (lane == 0)
    allow = jnp.concatenate([allow_rows, owner, own], axis=1).astype(f32)

    vmem = pl.BlockSpec(memory_space=pltpu.VMEM)
    smem = pl.BlockSpec(memory_space=pltpu.SMEM)
    dma = pltpu.SemaphoreType.DMA

    def scratch(*shape, dtype=f32):
        return pltpu.VMEM(shape, dtype)

    compact, summaries, rows = pl.pallas_call(
        kernel,
        name="decode",
        out_shape=(
            jax.ShapeDtypeStruct((4, PAGE, KVW), bf16),
            jax.ShapeDtypeStruct((8, KVW), bf16),
            jax.ShapeDtypeStruct((2, 8, 8, 8, 128), bf16),
        ),
        in_specs=[vmem] * 10 + [smem] + [vmem] * 7,
        out_specs=(vmem, vmem, vmem),
        scratch_shapes=[
            scratch(4, 32, 512, dtype=bf16),
            scratch(4, 16, 128, dtype=bf16),
            scratch(4, 16, 128, dtype=bf16),
            scratch(4, 16, 1024, dtype=bf16),
            scratch(4, 3, 16, 128, dtype=bf16),
            scratch(8, 4, 16, 128, dtype=bf16),
            scratch(8, 4, 16, 128, dtype=bf16),
            scratch(8, 4, 16, 1024, dtype=bf16),
            scratch(8, 2, 8, 16, 128, dtype=bf16),
            scratch(16, 2, 128),
            scratch(16, 2, 128),
            scratch(4, 4, 2, 128),
            scratch(32, 128),
            scratch(10, 64, 640, dtype=bf16),
            scratch(16, 640),
            scratch(4, 2 * QROWS, 128),
            scratch(4, 2, 512),
            scratch(16, 2, 512),
            scratch(32, 512),
            scratch(4, 32, 128),
            scratch(16, 32, 128, dtype=bf16),
            scratch(32, 128),
            scratch(4, 32, 256),
            scratch(4, 32, 256),
            scratch(16, 32, 128, dtype=bf16),
            scratch(4, 8, 128),
            scratch(4, 8, 128),
            scratch(2, 8, 8, 8, 128, dtype=bf16),
            scratch(8, 640),
            scratch(8, 1, 640),
            dma((4, 4)), dma((4,)),
            dma((2,)), dma((2,)),
            dma((2, 4, 2)), dma((2, 4, 2)),
            dma((13,)), dma((13,)),
        ],
        compiler_params=pltpu.CompilerParams(
            collective_id=0, has_side_effects=True, vmem_limit_bytes=48 << 20
        ),
    )(
        hidden_in, team[:, None], input_weight, output_weight, gate_weight, up_weight, down_weight,
        old_cache, keep_rows.T, drop_weights, inverse, cosine, sine, allow,
        attention_gain[None, :], feedforward_gain[None, :],
        jnp.tile(query_gain, 2)[None, :], jnp.tile(key_gain, 2)[None, :],
    )

    requests = hidden_in.shape[0]
    everyone = jnp.arange(requests, dtype=i32)
    position = everyone % R_DEV
    part = R_DEV // 2
    cont_index = everyone // R_DEV * part + position - part
    slot_of = source[jnp.clip(cont_index, 0, source.shape[0] - 1)]
    held_row = slot_of // part * R_DEV + part + slot_of % part
    row_of = jnp.where(position < part, everyone, held_row)
    ordered = rows.reshape(2, 4, 2, 8, 8, 128).transpose(3, 2, 0, 4, 1, 5).reshape(requests, 512)
    place = (row_of[:, None] == everyone[None, :]).astype(bf16)
    result = jnp.dot(place, ordered, preferred_element_type=f32).astype(bf16)
    return (compact, summaries, result)


def solution(mesh):
    placed = (
        P(None, "head"),
        P(),
        P(),
        P(),
        P(),
        P("req", "head"),
        P("req", "head"),
        P("req", "head"),
        P("req", "head"),
        P("req", "head"),
        P(("req", "head"), None, None),
        P(("req", "head"), None),
        P(("req", "head"), None),
        P(("req", "head"), None),
        P(),
        P("req", None),
        P(),
    )
    return jax.shard_map(
        on_device,
        mesh=mesh,
        in_specs=placed,
        out_specs=(P(("req", "head"), None, None), P(("req", "head"), None), P(None, "head")),
        check_vma=False,
    )
```

```python
import jax
import jax.numpy as jnp
import numpy as np
from jax import lax
from jax.experimental import pallas as pl
from jax.experimental.pallas import tpu as pltpu
from jax.sharding import PartitionSpec as P

D = 2048
HEADS = 20
KVH = 5
HD = 64
PAGE = 128
KEEP = 64
NP = 16
R_DEV = 2
KVW = 640
QROWS = 24

epsilon = 1e-06
negative = -1e30
bf16 = jnp.bfloat16
f32 = jnp.float32
i32 = jnp.int32


def iota(shape, dim):
    return lax.broadcasted_iota(i32, shape, dim)


def dot(a, b):
    return jnp.dot(a, b, preferred_element_type=f32)


def dot_t(a, b):
    return lax.dot_general(a, b, (((1,), (1,)), ((), ())), preferred_element_type=f32)


def rounded(values):
    return values.astype(bf16).astype(f32)


def at_lane(values, lane):
    return jnp.sum(jnp.where(iota(values.shape, 1) == lane, values, 0.0), axis=1, keepdims=True)


def kernel(
    hidden_hbm, win_hbm, wo_hbm, wg_hbm, wu_hbm, wd_hbm, cache_hbm, keep_hbm, drop_hbm, dest_hbm,
    lengths_hbm, table_hbm, source_hbm, again_hbm, fgain_hbm, qgain_hbm, kgain_hbm, turn_hbm,
    compact_ref, summary_ref, out_ref,
    hidden_ref, win_ref, wo_ref, wg_ref, wu_ref, wd_ref, cache_ref, keep_ref, drop_ref, dest_ref,
    lengths_ref, table_ref, source_ref, again_ref, fgain_ref, qgain_ref, kgain_ref, turn_ref,
    hx, win_s, wo_s, gu_s, wd_s, win_w, wo_w, gu_w, wd_w,
    pb, rb, cx, fa, kv, tail, dx, eb, ex, xa, ox, mx, mid_f, gs, gx, ax, ys, yx, jx, sumr, means,
    s_in, s_w1, r_w1, s_z, r_z, s_ring, r_ring, s_ph, r_ph, r_j,
):
    loads = [
        pltpu.make_async_copy(src, dst, s_in.at[k])
        for k, (src, dst) in enumerate((
            (win_hbm, win_ref), (source_hbm, source_ref), (hidden_hbm, hidden_ref), (wo_hbm, wo_ref),
            (wg_hbm, wg_ref), (wu_hbm, wu_ref), (wd_hbm, wd_ref), (keep_hbm, keep_ref),
            (drop_hbm, drop_ref), (cache_hbm, cache_ref), (dest_hbm, dest_ref), (lengths_hbm, lengths_ref),
            (table_hbm, table_ref), (again_hbm, again_ref), (fgain_hbm, fgain_ref), (qgain_hbm, qgain_ref),
            (kgain_hbm, kgain_ref), (turn_hbm, turn_ref),
        ))
    ]
    for load in loads:
        load.start()
    group = lax.axis_index("req")
    x = lax.axis_index("head")
    z = group // 16
    yc = lax.rem(group, 16)
    ya = yc // 4
    yb = lax.rem(yc, 4)
    y = yc // 2
    c = lax.rem(yc, 2)
    col = x * 4 + ya

    def dev(zz, yy, xx):
        return {"req": zz * 16 + yy, "head": xx}

    def remote(src, dst, ssem, rsem, target):
        return pltpu.make_async_remote_copy(
            src_ref=src, dst_ref=dst, send_sem=ssem, recv_sem=rsem,
            device_id=target, device_id_type=pl.DeviceIdType.MESH,
        )

    def yc_peer(j):
        return lax.rem(yc + j, 16)

    def col_peer(j):
        return lax.rem(col + j, 16)

    def x_peer(j):
        return lax.rem(x + j, 4)

    def yb_peer(j):
        return lax.rem(yb + j, 4)

    def z_peer(j):
        return lax.rem(z + j, 8)

    wd_w[:, :, 6:8] = jnp.zeros((8, 2, 2, 16, 128), bf16)

    barrier = pltpu.get_barrier_semaphore()

    def greet(target):
        pl.semaphore_signal(barrier, inc=1, device_id=target, device_id_type=pl.DeviceIdType.MESH)

    @pl.loop(1, 16)
    def _(j):
        greet(dev(z, yc_peer(j), x))

    for j in range(1, 4):
        greet(dev(z, yc, x_peer(j)))

    @pl.loop(1, 8)
    def _(j):
        greet(dev(z_peer(j), yc, x))

    for k in range(2):
        loads[k].wait()
    win = win_ref[...]
    pad = jnp.zeros((16, 32), bf16)
    even = jnp.concatenate([win, pad], axis=1)
    odd = jnp.concatenate([pad, win], axis=1)
    shifted = jnp.where(lax.rem(x, 2) == 0, even, odd)
    for a in range(4):
        win_s[a] = shifted[:, a * 128:(a + 1) * 128]

    source = source_ref[...].astype(f32)
    doubling = (iota((128, 256), 1) >> 1 == iota((128, 256), 0)).astype(bf16)
    source_of = dot(jnp.broadcast_to(source, (8, 128)).astype(bf16), doubling)

    def holds(rows, first):
        at = iota((rows, 256), 0)
        request = iota((rows, 256), 1)
        plain = ((at & 1) == 0) & (request == first + at)
        origin = jnp.broadcast_to(source_of[0:1], (rows, 256))
        carried = ((at & 1) == 1) & ((request & 1) == 1) & (origin == ((first + at) >> 1).astype(f32))
        return plain | carried

    chosen = jnp.where(holds(32, 32 * z), 1.0, 0.0).astype(bf16)
    loads[2].wait()
    hx[x] = dot(chosen, hidden_ref[...]).astype(bf16)

    pl.semaphore_wait(barrier, 25)

    def h_copy(j):
        return remote(hx.at[x], hx.at[x], s_ph.at[0], r_ph.at[0], dev(z, yc, x_peer(j)))

    cls = lax.rem(y, 4)
    yh = y // 4
    slot = yh * 2 + c

    def w1_parts(a):
        return (
            (win_s.at[a], win_w.at[z, slot], 0),
            (wo_s.at[a], wo_w.at[z, slot], 1),
            (gu_s.at[a], gu_w.at[z, slot], 2),
            (wd_s.at[a], wd_w.at[z, yh, pl.ds(c * 3, 3)], 3),
        )

    def w1_send(m):
        for a in range(4):
            src, dst, which = w1_parts(a)[m]
            target = a * 4 + cls

            @pl.when(target != yc)
            def _():
                remote(src, dst, s_w1.at[which, a], r_w1.at[which], dev(z, target, x)).start()

            @pl.when(target == yc)
            def _():
                pltpu.make_async_copy(src, dst, r_w1.at[which]).start()

    def w1_wait(which, block):
        pltpu.make_async_copy(block, block, r_w1.at[which]).wait()

    def z_copy(which, buf, j):
        return remote(buf.at[z], buf.at[z], s_z.at[which], r_z.at[which], dev(z_peer(j), yc, x))

    def seven(buf):
        return buf.at[pl.ds(0, 7)]

    w1_send(0)
    for j in range(1, 4):
        h_copy(j).start()

    for k in range(3, 7):
        loads[k].wait()
    wo_full = jnp.concatenate([wo_ref[...], jnp.zeros((6, 512), bf16)], axis=0)
    wd_full = jnp.concatenate([wd_ref[...], jnp.zeros((8, 512), bf16)], axis=0)
    gu_s[...] = jnp.zeros_like(gu_s)
    gate = wg_ref[...]
    up = wu_ref[...]
    for a in range(4):
        lanes = slice(a * 128, (a + 1) * 128)
        wo_s[a] = wo_full[:, lanes]
        for k in range(3):
            wd_s[a, k] = wd_full[k * 16:(k + 1) * 16, lanes]
        for k in range(4):
            for h in range(2):
                first = a * 320 + k * 80 + h * 40
                gu_s[a, :, k * 256 + h * 48:k * 256 + h * 48 + 40] = gate[:, first:first + 40]
                gu_s[a, :, k * 256 + 128 + h * 48:k * 256 + 128 + h * 48 + 40] = up[:, first:first + 40]
    for m in range(1, 4):
        w1_send(m)

    def ring(step, way, which):
        block = lax.rem(z - (step - 1) + 8, 8) if way == 0 else lax.rem(z + step - 1, 8)
        target = lax.rem(z + 1, 8) if way == 0 else lax.rem(z + 7, 8)
        ref = gu_w.at[block] if which == 0 else wd_w.at[block, :, pl.ds(0, 6)]
        return remote(ref, ref, s_ring.at[way, step - 1, which], r_ring.at[way, step - 1, which], dev(target, yc, x))

    def ways(step):
        return (0, 1) if step < 4 else (0,)

    def ring_step(step):
        for which in range(2):
            for way in (0, 1):
                if step > 1 and way in ways(step - 1):
                    ring(step - 1, way, which).wait_recv()
            if step <= 4:
                for way in ways(step):
                    ring(step, way, which).start()

    for k in range(7, 18):
        loads[k].wait()
    bias = jnp.zeros((1, 640), f32)
    tail[...] = jnp.zeros_like(tail)
    lane640 = iota((1, 640), 1)
    row_ids = iota((64, 128), 1).astype(f32)
    eye = (iota((64, 64), 0) == iota((64, 64), 1)).astype(bf16)
    keep_all = dot_t(eye, keep_ref[...].astype(f32).astype(bf16))

    def compact_page(p, bias):
        picks = (keep_all[:, p:p + 1] == row_ids).astype(f32)
        weight = drop_ref[p:p + 1, :] * (1.0 - jnp.sum(picks, axis=0, keepdims=True))
        total = jnp.sum(weight, axis=1, keepdims=True)
        w1 = rounded(weight)
        w2 = rounded(weight - w1)
        w3 = weight - w1 - w2
        left = jnp.concatenate([picks, w1, w2, w3, jnp.zeros((13, 128), f32)], axis=0).astype(bf16)
        got = dot(left, cache_ref[p])
        kv[p] = got[0:64].astype(bf16)
        mean = rounded((got[64:65] + got[65:66] + got[66:67]) / total)
        tail[p:p + 1, :] = mean
        means[p] = mean
        return jnp.where(lane640 == 512 + p, jnp.log(total), bias)

    for p in range(4):
        bias = compact_page(p, bias)

    w1_wait(0, win_w.at[z])

    @pl.loop(1, 8)
    def _(j):
        z_copy(0, win_w, j).start()

    w1_wait(1, wo_w.at[z])

    @pl.loop(1, 8)
    def _(j):
        z_copy(1, wo_w, j).start()

    for p in range(4, 8):
        bias = compact_page(p, bias)

    w1_wait(2, gu_w.at[z])
    w1_wait(3, wd_w.at[z, :, pl.ds(0, 6)])
    ring_step(1)

    own_len = jnp.sum(
        jnp.where(holds(8, 2 * group), jnp.broadcast_to(lengths_ref[...].astype(f32), (8, 256)), 0.0),
        axis=1, keepdims=True,
    )[0:2]
    cos2 = jnp.zeros((2, 128), f32)
    sin2 = jnp.zeros((2, 128), f32)
    for k in range(NP):
        cos2 = jnp.where(own_len == k + 1.0, turn_ref[k:k + 1, :], cos2)
        sin2 = jnp.where(own_len == k + 1.0, turn_ref[NP + k:NP + k + 1, :], sin2)
    table = table_ref[...].astype(f32)
    entry = iota((2, 640), 1)
    page_of = jnp.where(entry < 512, entry >> 6, entry - 512).astype(f32)
    owned = jnp.zeros((2, 640), f32)
    for k in range(4):
        logical = 4 * k + x
        spot_of = jnp.sum(jnp.where(iota((2, NP), 1) == logical, table, 0.0), axis=1, keepdims=True)
        alive = jnp.where(own_len > logical.astype(f32), 1.0, 0.0)
        owned = jnp.where(page_of == spot_of, alive, owned)
    listed = jnp.concatenate(
        [keep_ref[k:k + 1, :] for k in range(8)] + [jnp.zeros((1, 128), i32)], axis=1
    )
    owned = jnp.where((entry < 520) & (listed >= 0), owned, 0.0)
    allow = jnp.where((entry == 520 + iota((2, 640), 0)) & (x == 0), 1.0, owned)

    sel_row = iota((512, 128), 0)
    sel_col = iota((512, 128), 1)
    select = (
        ((sel_row & 127) >> 5 == yb)
        & (sel_col >> 5 == sel_row >> 7)
        & ((sel_row & 31) == (sel_col & 31))
    ).astype(bf16)

    pltpu.make_async_copy(hx.at[pl.ds(0, 3)], hx.at[pl.ds(0, 3)], r_ph.at[0]).wait()
    square = jnp.zeros((32, 1), f32)
    for k in range(4):
        part = hx[k].astype(f32)
        square += jnp.sum(part * part, axis=1, keepdims=True)
    scale = lax.rsqrt(square * (1.0 / D) + epsilon)
    pieces = []
    for k in range(4):
        normed = (hx[k].astype(f32) * scale * again_ref[:, k * 512:(k + 1) * 512]).astype(bf16)
        pieces.append(dot(normed, select).astype(bf16))
    x_in = jnp.concatenate(pieces, axis=1)

    pltpu.make_async_copy(seven(win_w), seven(win_w), r_z.at[0]).wait()
    partial = dot(x_in, win_w[...].reshape(512, 128))
    for k in range(16):
        pb[k] = partial[2 * k:2 * k + 2, :]
    rb[yc] = pb[yc]

    def b_copy(j):
        return remote(pb.at[yc_peer(j)], rb.at[yc], s_ph.at[1], r_ph.at[1], dev(z, yc_peer(j), x))

    @pl.loop(1, 16)
    def _(j):
        b_copy(j).start()

    ring_step(2)
    fifteen = pl.ds(0, 15)
    pltpu.make_async_copy(rb.at[fifteen], rb.at[fifteen], r_ph.at[1]).wait()
    for a in range(4):
        cx[x, a] = rounded(rb[4 * a] + rb[4 * a + 1] + rb[4 * a + 2] + rb[4 * a + 3])

    def c_copy(j):
        return remote(cx.at[x], cx.at[x], s_ph.at[2], r_ph.at[2], dev(z, yc, x_peer(j)))

    for j in range(1, 4):
        c_copy(j).start()
    three = pl.ds(0, 3)
    pltpu.make_async_copy(cx.at[three], cx.at[three], r_ph.at[2]).wait()
    for k in range(16):
        fa[2 * k:2 * k + 2, :] = cx[k // 4, k % 4]

    mixed = fa[...]
    row = iota((32, 128), 0)
    lane = iota((32, 128), 1)
    low = lane < 64
    block = row >> 1
    moved = pltpu.roll(pltpu.roll(mixed, 30, 0), 64, 1)
    mixed = jnp.where(((block == 3) | (block == 11)) & ~low, mixed + moved, mixed)
    sq = mixed * mixed
    ms_low = jnp.sum(jnp.where(low, sq, 0.0), axis=1, keepdims=True) * (1.0 / HD)
    ms_high = jnp.sum(jnp.where(low, 0.0, sq), axis=1, keepdims=True) * (1.0 / HD)
    inverse = jnp.where(low, lax.rsqrt(ms_low + epsilon), lax.rsqrt(ms_high + epsilon))
    place = block * 2 + jnp.where(low, 0, 1)
    qgain = jnp.concatenate([qgain_ref[...]] * 2, axis=1)
    kgain = jnp.concatenate([kgain_ref[...]] * 2, axis=1)
    gain = jnp.where(place <= 20, qgain, kgain)
    vec = mixed * inverse * gain
    even_row = (row & 1) == 0
    cosine = jnp.where(even_row, cos2[0:1, :], cos2[1:2, :])
    sine = jnp.where(even_row, sin2[0:1, :], sin2[1:2, :])
    first_half = (lane & 63) < 32
    rotated = jnp.where(
        first_half,
        vec * cosine - pltpu.roll(vec, 96, 1) * sine,
        vec * cosine + pltpu.roll(vec, 32, 1) * sine,
    )
    final = jnp.where(place >= 27, mixed, rounded(rotated))
    swapped = pltpu.roll(final, 64, 1)
    low2 = low[0:2]

    def two(values, b):
        return values[2 * b:2 * b + 2, :]

    tail[8:10, 0:128] = jnp.where(low2, two(swapped, 10), two(swapped, 11))
    tail[8:10, 128:256] = jnp.where(low2, two(swapped, 11), two(final, 12))
    tail[8:10, 256:384] = two(final, 13)
    tail[8:10, 384:512] = two(final, 14)
    tail[8:10, 512:640] = two(final, 15)
    kv[8, 0:16] = tail[...].astype(bf16)
    kv[8, 16:64] = jnp.zeros((48, 640), bf16)
    kv[9] = jnp.zeros((64, 640), bf16)

    lowq = low[0:QROWS]
    fq = final[0:QROWS]
    gq = swapped[0:QROWS]
    both = jnp.concatenate([jnp.where(lowq, fq, gq), jnp.where(lowq, gq, fq)], axis=0)
    nrow = 2 * QROWS

    def row_facts(width):
        at = iota((nrow, width), 0)
        second = at >= QROWS
        inside = jnp.where(second, at - QROWS, at)
        request = inside & 1
        spot = (inside >> 1) * 2 + jnp.where(second, 1, 0)
        head = jnp.where(spot <= 7, spot, spot - 1)
        valid = (spot != 8) & (spot <= 20)
        return request, head, valid

    request, head, valid = row_facts(384)
    lane384 = iota((nrow, 384), 1)
    queries = jnp.where(
        valid & (lane384 >> 6 == head >> 2), jnp.concatenate([both, both, both], axis=1), 0.0
    ).astype(bf16)
    scores = dot_t(queries, kv[:, :, 0:384].reshape(640, 384)) * (HD ** (-0.5)) + bias
    request640, _, _ = row_facts(640)
    permit = jnp.where(request640 == 0, allow[0:1, :], allow[1:2, :]) > 0.5
    scores = jnp.where(permit, scores, negative)
    top = jnp.max(scores, axis=1, keepdims=True)
    weight = jnp.where(permit, jnp.exp(scores - top), 0.0)
    mass = jnp.sum(weight, axis=1, keepdims=True)
    w1 = rounded(weight)
    w2 = rounded(weight - w1)
    w3 = weight - w1 - w2
    summed = dot(jnp.concatenate([w1, w2, w3], axis=0).astype(bf16), kv[:, :, 256:640].reshape(640, 384))
    summed = summed[0:nrow] + summed[nrow:2 * nrow] + summed[2 * nrow:3 * nrow]
    summed = jnp.where(lane384 >> 6 == (head >> 2) + 1, summed, 0.0)
    folded = summed[:, 0:128] + summed[:, 128:256] + summed[:, 256:384]
    folded = folded + pltpu.roll(folded, 64, 1)
    lane128 = iota((nrow, 128), 1)
    dx[x] = jnp.where(
        lane128 < 64, folded, jnp.where(lane128 == 64, mass, jnp.where(lane128 == 65, top, 0.0))
    )

    def d_copy(j):
        return remote(dx.at[x], dx.at[x], s_ph.at[3], r_ph.at[3], dev(z, yc, x_peer(j)))

    for j in range(1, 4):
        d_copy(j).start()
    ring_step(3)

    for f in range(8):
        page = 0
        for q in range(1, 8):
            page = jnp.where(dest_ref[0, q] == f, q, page)
        compact_ref[f // 2, (f % 2) * 64:(f % 2) * 64 + 64, :] = kv[page]
        sumr[f:f + 1, :] = means[page]
    summary_ref[...] = sumr[...].astype(bf16)

    kap = iota((1, 2048), 1)
    kclass = kap >> 9
    kz = (kap >> 6) & 7
    kyh = (kap >> 5) & 1
    kc = (kap >> 4) & 1
    ki = kap & 15
    feature = 10 * (kz * 16 + (4 * kyh + kclass) * 2 + kc) + ki
    real = ki < 10
    spread = (((feature & 63) == iota((128, 2048), 0)) & real).astype(bf16)

    pltpu.make_async_copy(dx.at[three], dx.at[three], r_ph.at[3]).wait()
    parts = [dx[k] for k in range(4)]
    tops = [at_lane(part, 65) for part in parts]
    best = jnp.maximum(jnp.maximum(tops[0], tops[1]), jnp.maximum(tops[2], tops[3]))
    acc = jnp.zeros((nrow, 128), f32)
    for k in range(4):
        acc += parts[k] * jnp.exp(tops[k] - best)
    attention = jnp.where(lane128 < 64, acc / at_lane(acc, 64), 0.0).astype(bf16)
    _, head2048, valid2048 = row_facts(2048)
    spread_rows = dot(attention, spread)
    spread_rows = jnp.where(valid2048 & (head2048 == feature >> 6), spread_rows, 0.0).astype(bf16)
    pick_at = iota((8, nrow), 1)
    pick_second = jnp.where(pick_at >= QROWS, pick_at - QROWS, pick_at)
    pick = ((pick_second & 1) == iota((8, nrow), 0)).astype(bf16)
    grouped = dot(pick, spread_rows)
    for k in range(4):
        eb[k] = grouped[0:2, k * 512:(k + 1) * 512]
    ex[yc] = eb[yb]

    def e_copy(j):
        return remote(
            eb.at[lax.rem(yc_peer(j), 4)], ex.at[yc], s_ph.at[4], r_ph.at[4], dev(z, yc_peer(j), x)
        )

    @pl.loop(1, 16)
    def _(j):
        e_copy(j).start()

    ring_step(4)
    pltpu.make_async_copy(seven(wo_w), seven(wo_w), r_z.at[1]).wait()
    pltpu.make_async_copy(ex.at[fifteen], ex.at[fifteen], r_ph.at[4]).wait()
    for k in range(16):
        xa[2 * k:2 * k + 2, :] = ex[k]
    ox[yb] = dot(xa[...].astype(bf16), wo_w[...].reshape(512, 128))

    def o_copy(j):
        return remote(ox.at[yb], ox.at[yb], s_ph.at[5], r_ph.at[5], dev(z, ya * 4 + yb_peer(j), x))

    for j in range(1, 4):
        o_copy(j).start()
    pltpu.make_async_copy(ox.at[three], ox.at[three], r_ph.at[5]).wait()
    residual = jnp.zeros((32, 128), f32)
    own_rows = hx[x]
    for k in range(4):
        residual = jnp.where(ya == k, own_rows[:, k * 128:(k + 1) * 128].astype(f32), residual)
    mid = (residual + (ox[0] + ox[1] + ox[2] + ox[3])).astype(bf16)
    mx[col] = mid
    mid_f[...] = mid.astype(f32)

    def m_copy(buf, n, j):
        peer = col_peer(j)
        return remote(
            buf.at[col], buf.at[col], s_ph.at[n], r_ph.at[n], dev(z, lax.rem(peer, 4) * 4 + yb, peer // 4)
        )

    @pl.loop(1, 16)
    def _(j):
        m_copy(mx, 6, j).start()

    pltpu.make_async_copy(mx.at[fifteen], mx.at[fifteen], r_ph.at[6]).wait()
    square = jnp.zeros((32, 128), f32)
    for k in range(16):
        part = mx[k].astype(f32)
        square += part * part
    scale = lax.rsqrt(jnp.sum(square, axis=1, keepdims=True) * (1.0 / D) + epsilon)
    pieces = []
    for u in range(4):
        tiles = []
        for t in range(4):
            k = 4 * u + t
            tiles.append((mx[k].astype(f32) * scale * fgain_ref[:, k * 128:(k + 1) * 128]).astype(bf16))
        pieces.append(dot(jnp.concatenate(tiles, axis=1), select).astype(bf16))
    x_mid = jnp.concatenate(pieces, axis=1)

    ring_step(5)
    for k in range(4):
        gs[k] = dot(x_mid, gu_w[:, :, :, k * 256:(k + 1) * 256].reshape(512, 256))
    gx[yb] = gs[yb]

    def g_copy(j):
        return remote(gs.at[yb_peer(j)], gx.at[yb], s_ph.at[7], r_ph.at[7], dev(z, ya * 4 + yb_peer(j), x))

    for j in range(1, 4):
        g_copy(j).start()
    pltpu.make_async_copy(gx.at[three], gx.at[three], r_ph.at[7]).wait()
    sums = gx[0] + gx[1] + gx[2] + gx[3]
    gate_sum = sums[:, 0:128]
    ax[col] = (gate_sum / (1.0 + jnp.exp(-gate_sum)) * sums[:, 128:256]).astype(bf16)

    @pl.loop(1, 16)
    def _(j):
        m_copy(ax, 8, j).start()

    pltpu.make_async_copy(ax.at[fifteen], ax.at[fifteen], r_ph.at[8]).wait()
    whole = jnp.concatenate([ax[k] for k in range(16)], axis=1)
    down = dot(whole, wd_w[...].reshape(2048, 128))
    for k in range(4):
        ys[k] = down[8 * k:8 * k + 8, :]
    yx[yb] = ys[yb]

    def y_copy(j):
        return remote(ys.at[yb_peer(j)], yx.at[yb], s_ph.at[9], r_ph.at[9], dev(z, ya * 4 + yb_peer(j), x))

    for j in range(1, 4):
        y_copy(j).start()
    pltpu.make_async_copy(yx.at[three], yx.at[three], r_ph.at[9]).wait()
    mine = mid_f[pl.ds(pl.multiple_of(yb * 8, 8), 8), :]
    outer = jnp.where(c == 0, y, z)
    inner = jnp.where(c == 0, z, y)
    jx[c, outer, inner] = (mine + (yx[0] + yx[1] + yx[2] + yx[3])).astype(bf16)

    def along(value, first):
        zz = jnp.where((c == 0) == first, value, z)
        yy = jnp.where((c == 0) == first, y, value)
        return dev(zz, yy * 2 + c, x)

    mate = dev(z, y * 2 + 1 - c, x)

    @pl.loop(1, 8)
    def _(j):
        block = jx.at[c, outer, inner]
        remote(block, block, s_ph.at[10], r_ph.at[10], along(lax.rem(inner + j, 8), True)).start()

    pltpu.make_async_copy(jx.at[0, 0, pl.ds(0, 7)], jx.at[0, 0, pl.ds(0, 7)], r_ph.at[10]).wait()

    def j_copy(j):
        block = jx.at[c, outer]
        return remote(block, block, s_ph.at[11], r_j.at[outer], along(lax.rem(outer + j, 8), False))

    def m_forward(at):
        block = jx.at[c, at]
        return remote(block, block, s_ph.at[12], r_ph.at[12], mate)

    @pl.loop(1, 8)
    def _(j):
        j_copy(j).start()

    m_forward(outer).start()

    into = (iota((256, 128), 0) >> 1 == iota((256, 128), 1)).astype(bf16)
    group_of = dot_t(into, jnp.broadcast_to(source, (8, 128)).astype(bf16))[:, 0:1]
    request_id = iota((256, 256), 0)
    spot = iota((256, 256), 1)
    held_row = ((spot >> 3) & 7) * 32 + (spot >> 7) * 16 + ((spot >> 6) & 1) * 8 + (spot & 7)
    wanted = jnp.where((request_id & 1) == 0, request_id.astype(f32), 2.0 * group_of + 1.0)
    back = (held_row.astype(f32) == wanted).astype(bf16)

    @pl.loop(1, 8)
    def _(j):
        at = lax.rem(outer + 8 - j, 8)
        block = jx.at[c, at]
        remote(block, block, s_ph.at[11], r_j.at[at], mate).wait_recv()
        m_forward(at).start()

    pltpu.make_async_copy(jx.at[0], jx.at[0], r_ph.at[12]).wait()
    for a in range(4):
        blocks = []
        for h in range(2):
            blocks.append(jx[0, 2 * a + h].reshape(64, 128))
            blocks.append(jx[1, :, 2 * a + h].reshape(64, 128))
        out_ref[:, a * 128:(a + 1) * 128] = dot(back, jnp.concatenate(blocks, axis=0)).astype(bf16)


    def sent(block, sem):
        pltpu.make_async_copy(block, block, sem).wait()

    for m in range(4):
        for a in range(4):
            src, dst, which = w1_parts(a)[m]
            target = a * 4 + cls

            @pl.when(target != yc)
            def _():
                remote(src, dst, s_w1.at[which, a], r_w1.at[which], dev(z, target, x)).wait_send()

    sent(seven(win_w), s_z.at[0])
    sent(seven(wo_w), s_z.at[1])
    for step in range(1, 5):
        for which in range(2):
            for way in ways(step):
                ring(step, way, which).wait_send()
    sent(hx.at[three], s_ph.at[0])
    sent(rb.at[fifteen], s_ph.at[1])
    sent(cx.at[three], s_ph.at[2])
    sent(dx.at[three], s_ph.at[3])
    sent(ex.at[fifteen], s_ph.at[4])
    sent(ox.at[three], s_ph.at[5])
    sent(mx.at[fifteen], s_ph.at[6])
    sent(gx.at[three], s_ph.at[7])
    sent(ax.at[fifteen], s_ph.at[8])
    sent(yx.at[three], s_ph.at[9])
    sent(jx.at[0, 0, pl.ds(0, 7)], s_ph.at[10])
    sent(jx.at[0, pl.ds(0, 7)], s_ph.at[11])
    sent(jx.at[0], s_ph.at[12])


def rotation_table():
    half = HD // 2
    frequency = np.float32(10000.0) ** (-np.arange(half, dtype=np.float32) / np.float32(half))
    positions = (PAGE * np.arange(1, NP + 1)).astype(np.float32)
    angles = np.tile((positions[:, None] * frequency[None, :]).astype(np.float64), (1, 4))
    return np.concatenate([np.cos(angles), np.sin(angles)], axis=0).astype(np.float32)


def on_device(
    hidden_in, attention_gain, query_gain, key_gain, feedforward_gain,
    input_weight, output_weight, gate_weight, up_weight, down_weight,
    old_cache, keep_rows, drop_weights, dest_slots, lengths, page_table, source,
):
    operands = (
        hidden_in, input_weight, output_weight, gate_weight, up_weight, down_weight,
        old_cache, keep_rows, drop_weights, dest_slots,
        lengths[None, :], page_table, source[None, :],
        attention_gain[None, :], feedforward_gain[None, :], query_gain[None, :], key_gain[None, :],
        jnp.asarray(rotation_table()),
    )
    vmem = pl.BlockSpec(memory_space=pltpu.VMEM)
    hbm = pl.BlockSpec(memory_space=pltpu.HBM)
    dma = pltpu.SemaphoreType.DMA

    def scratch(*shape, dtype=f32):
        return pltpu.VMEM(shape, dtype)

    return pl.pallas_call(
        kernel,
        name="decode",
        out_shape=(
            jax.ShapeDtypeStruct((4, PAGE, KVW), bf16),
            jax.ShapeDtypeStruct((8, KVW), bf16),
            jax.ShapeDtypeStruct(hidden_in.shape, bf16),
        ),
        in_specs=[hbm] * len(operands),
        out_specs=(vmem, vmem, vmem),
        scratch_shapes=[
            (pltpu.SMEM if k == 9 else pltpu.VMEM)(a.shape, a.dtype) for k, a in enumerate(operands)
        ] + [
            scratch(4, 32, 512, dtype=bf16),
            scratch(4, 16, 128, dtype=bf16),
            scratch(4, 16, 128, dtype=bf16),
            scratch(4, 16, 1024, dtype=bf16),
            scratch(4, 3, 16, 128, dtype=bf16),
            scratch(8, 4, 16, 128, dtype=bf16),
            scratch(8, 4, 16, 128, dtype=bf16),
            scratch(8, 4, 16, 1024, dtype=bf16),
            scratch(8, 2, 8, 16, 128, dtype=bf16),
            scratch(16, 2, 128),
            scratch(16, 2, 128),
            scratch(4, 4, 2, 128),
            scratch(32, 128),
            scratch(10, 64, 640, dtype=bf16),
            scratch(16, 640),
            scratch(4, 2 * QROWS, 128),
            scratch(4, 2, 512),
            scratch(16, 2, 512),
            scratch(32, 512),
            scratch(4, 32, 128),
            scratch(16, 32, 128, dtype=bf16),
            scratch(32, 128),
            scratch(4, 32, 256),
            scratch(4, 32, 256),
            scratch(16, 32, 128, dtype=bf16),
            scratch(4, 8, 128),
            scratch(4, 8, 128),
            scratch(2, 8, 8, 8, 128, dtype=bf16),
            scratch(8, 640),
            scratch(8, 1, 640),
            dma((len(operands),)),
            dma((4, 4)), dma((4,)),
            dma((2,)), dma((2,)),
            dma((2, 4, 2)), dma((2, 4, 2)),
            dma((13,)), dma((13,)), dma((8,)),
        ],
        compiler_params=pltpu.CompilerParams(
            collective_id=0, has_side_effects=True, vmem_limit_bytes=63 << 20
        ),
    )(*operands)


def solution(mesh):
    placed = (
        P(None, "head"),
        P(),
        P(),
        P(),
        P(),
        P("req", "head"),
        P("req", "head"),
        P("req", "head"),
        P("req", "head"),
        P("req", "head"),
        P(("req", "head"), None, None),
        P(("req", "head"), None),
        P(("req", "head"), None),
        P(("req", "head"), None),
        P(),
        P("req", None),
        P(),
    )
    return jax.shard_map(
        on_device,
        mesh=mesh,
        in_specs=placed,
        out_specs=(P(("req", "head"), None, None), P(("req", "head"), None), P(None, "head")),
        check_vma=False,
    )
```

```python
import jax
import jax.numpy as jnp
import numpy as np
from jax import lax
from jax.experimental import pallas as pl
from jax.experimental.pallas import tpu as pltpu
from jax.sharding import PartitionSpec as P

D = 2048
HEADS = 20
KVH = 5
HD = 64
PAGE = 128
KEEP = 64
NP = 16
R_DEV = 2
KVW = 640
QROWS = 24

epsilon = 1e-06
negative = -1e30
bf16 = jnp.bfloat16
f32 = jnp.float32
i32 = jnp.int32


def iota(shape, dim):
    return lax.broadcasted_iota(i32, shape, dim)


def dot(a, b):
    return jnp.dot(a, b, preferred_element_type=f32)


def dot_t(a, b):
    return lax.dot_general(a, b, (((1,), (1,)), ((), ())), preferred_element_type=f32)


def rounded(values):
    return values.astype(bf16).astype(f32)


def at_lane(values, lane):
    return jnp.sum(jnp.where(iota(values.shape, 1) == lane, values, 0.0), axis=1, keepdims=True)


def kernel(
    hidden_hbm, win_hbm, wo_hbm, wg_hbm, wu_hbm, wd_hbm, cache_hbm, keep_hbm, drop_hbm, dest_hbm,
    lengths_hbm, table_hbm, source_hbm, again_hbm, fgain_hbm, qgain_hbm, kgain_hbm, turn_hbm,
    compact_hbm, summary_hbm, out_hbm,
    hidden_ref, win_ref, wo_ref, wg_ref, wu_ref, wd_ref, cache_ref, keep_ref, drop_ref, dest_ref,
    lengths_ref, table_ref, source_ref, again_ref, fgain_ref, qgain_ref, kgain_ref, turn_ref,
    hx, win_s, wo_s, gu_s, wd_s, win_w, wo_w, gu_w, wd_w,
    pb, rb, cx, fa, kv, tail, dx, eb, ex, xa, ox, mx, mid_f, ax, ys, yx, jx, sumr, means, compact_ref, summary_ref, out_ref,
    s_in, s_out, s_w1, r_w1, s_z, r_z, s_ring, r_ring, s_ph, r_ph, r_j,
):
    loads = [
        pltpu.make_async_copy(src, dst, s_in.at[k])
        for k, (src, dst) in enumerate((
            (win_hbm, win_ref), (source_hbm, source_ref), (hidden_hbm, hidden_ref), (wo_hbm, wo_ref),
            (wg_hbm, wg_ref), (wu_hbm, wu_ref), (wd_hbm, wd_ref), (keep_hbm, keep_ref),
            (drop_hbm, drop_ref), (cache_hbm, cache_ref), (dest_hbm, dest_ref), (lengths_hbm, lengths_ref),
            (table_hbm, table_ref), (again_hbm, again_ref), (fgain_hbm, fgain_ref), (qgain_hbm, qgain_ref),
            (kgain_hbm, kgain_ref), (turn_hbm, turn_ref),
        ))
    ]
    for load in loads:
        load.start()
    group = lax.axis_index("req")
    x = lax.axis_index("head")
    z = group // 16
    yc = lax.rem(group, 16)
    ya = yc // 4
    yb = lax.rem(yc, 4)
    y = yc // 2
    c = lax.rem(yc, 2)
    col = x * 4 + ya

    def dev(zz, yy, xx):
        return {"req": zz * 16 + yy, "head": xx}

    def remote(src, dst, ssem, rsem, target):
        return pltpu.make_async_remote_copy(
            src_ref=src, dst_ref=dst, send_sem=ssem, recv_sem=rsem,
            device_id=target, device_id_type=pl.DeviceIdType.MESH,
        )

    def yc_peer(j):
        return lax.rem(yc + j, 16)

    def col_peer(j):
        return lax.rem(col + j, 16)

    def x_peer(j):
        return lax.rem(x + j, 4)

    def yb_peer(j):
        return lax.rem(yb + j, 4)

    def z_peer(j):
        return lax.rem(z + j, 8)

    wd_w[:, :, 6:8] = jnp.zeros((8, 2, 2, 16, 128), bf16)

    barrier = pltpu.get_barrier_semaphore()

    def greet(target):
        pl.semaphore_signal(barrier, inc=1, device_id=target, device_id_type=pl.DeviceIdType.MESH)

    @pl.loop(1, 16)
    def _(j):
        greet(dev(z, yc_peer(j), x))

    for j in range(1, 4):
        greet(dev(z, yc, x_peer(j)))

    @pl.loop(1, 8)
    def _(j):
        greet(dev(z_peer(j), yc, x))

    for k in range(2):
        loads[k].wait()
    win = win_ref[...]
    pad = jnp.zeros((16, 32), bf16)
    even = jnp.concatenate([win, pad], axis=1)
    odd = jnp.concatenate([pad, win], axis=1)
    shifted = jnp.where(lax.rem(x, 2) == 0, even, odd)
    for a in range(4):
        win_s[a] = shifted[:, a * 128:(a + 1) * 128]

    source = source_ref[...].astype(f32)
    doubling = (iota((128, 256), 1) >> 1 == iota((128, 256), 0)).astype(bf16)
    source_of = dot(jnp.broadcast_to(source, (8, 128)).astype(bf16), doubling)

    def holds(rows, first):
        at = iota((rows, 256), 0)
        request = iota((rows, 256), 1)
        plain = ((at & 1) == 0) & (request == first + at)
        origin = jnp.broadcast_to(source_of[0:1], (rows, 256))
        carried = ((at & 1) == 1) & ((request & 1) == 1) & (origin == ((first + at) >> 1).astype(f32))
        return plain | carried

    chosen = jnp.where(holds(32, 32 * z), 1.0, 0.0).astype(bf16)
    loads[2].wait()
    hx[x] = dot(chosen, hidden_ref[...]).astype(bf16)

    pl.semaphore_wait(barrier, 25)

    def h_copy(j):
        return remote(hx.at[x], hx.at[x], s_ph.at[0], r_ph.at[0], dev(z, yc, x_peer(j)))

    cls = lax.rem(y, 4)
    yh = y // 4
    slot = yh * 2 + c

    def w1_parts(a):
        return (
            (win_s.at[a], win_w.at[z, slot], 0),
            (wo_s.at[a], wo_w.at[z, slot], 1),
            (wd_s.at[a], wd_w.at[z, yh, pl.ds(c * 3, 3)], 2),
        )

    def w1_send(m):
        for a in range(4):
            src, dst, which = w1_parts(a)[m]
            target = a * 4 + cls

            @pl.when(target != yc)
            def _():
                remote(src, dst, s_w1.at[which, a], r_w1.at[which], dev(z, target, x)).start()

            @pl.when(target == yc)
            def _():
                pltpu.make_async_copy(src, dst, r_w1.at[which]).start()

    def w1_wait(which, block):
        pltpu.make_async_copy(block, block, r_w1.at[which]).wait()

    def z_copy(which, buf, j):
        return remote(buf.at[z], buf.at[z], s_z.at[which], r_z.at[which], dev(z_peer(j), yc, x))

    def seven(buf):
        return buf.at[pl.ds(0, 7)]

    w1_send(0)
    for j in range(1, 4):
        h_copy(j).start()

    for k in range(3, 7):
        loads[k].wait()
    wo_full = jnp.concatenate([wo_ref[...], jnp.zeros((6, 512), bf16)], axis=0)
    wd_full = jnp.concatenate([wd_ref[...], jnp.zeros((8, 512), bf16)], axis=0)
    gu_s[...] = jnp.zeros_like(gu_s)
    gate = wg_ref[...]
    up = wu_ref[...]
    for a in range(4):
        lanes = slice(a * 128, (a + 1) * 128)
        wo_s[a] = wo_full[:, lanes]
        for k in range(3):
            wd_s[a, k] = wd_full[k * 16:(k + 1) * 16, lanes]
        for k in range(4):
            for h in range(2):
                first = a * 320 + k * 80 + h * 40
                gu_s[a * 4 + k, :, h * 48:h * 48 + 40] = gate[:, first:first + 40]
                gu_s[a * 4 + k, :, 128 + h * 48:128 + h * 48 + 40] = up[:, first:first + 40]
    w1_send(1)
    gu_w[z, yc] = gu_s[yc]

    def gu_copy(j):
        return remote(gu_s.at[yc_peer(j)], gu_w.at[z, yc], s_ph.at[7], r_ph.at[7], dev(z, yc_peer(j), x))


    def ring(step, way, which):
        block = lax.rem(z - (step - 1) + 8, 8) if way == 0 else lax.rem(z + step - 1, 8)
        target = lax.rem(z + 1, 8) if way == 0 else lax.rem(z + 7, 8)
        ref = gu_w.at[block] if which == 0 else wd_w.at[block, :, pl.ds(0, 6)]
        return remote(ref, ref, s_ring.at[way, step - 1, which], r_ring.at[way, step - 1, which], dev(target, yc, x))

    def ways(step):
        return (0, 1) if step < 4 else (0,)

    def ring_step(step):
        for which in range(2):
            for way in (0, 1):
                if step > 1 and way in ways(step - 1):
                    ring(step - 1, way, which).wait_recv()
            if step <= 4:
                for way in ways(step):
                    ring(step, way, which).start()

    for k in range(7, 18):
        loads[k].wait()
    bias = jnp.zeros((1, 640), f32)
    tail[...] = jnp.zeros_like(tail)
    lane640 = iota((1, 640), 1)
    row_ids = iota((64, 128), 1).astype(f32)
    eye = (iota((64, 64), 0) == iota((64, 64), 1)).astype(bf16)
    keep_all = dot_t(eye, keep_ref[...].astype(f32).astype(bf16))

    def compact_page(p, bias):
        picks = (keep_all[:, p:p + 1] == row_ids).astype(f32)
        weight = drop_ref[p:p + 1, :] * (1.0 - jnp.sum(picks, axis=0, keepdims=True))
        total = jnp.sum(weight, axis=1, keepdims=True)
        w1 = rounded(weight)
        w2 = rounded(weight - w1)
        w3 = weight - w1 - w2
        left = jnp.concatenate([picks, w1, w2, w3, jnp.zeros((13, 128), f32)], axis=0).astype(bf16)
        got = dot(left, cache_ref[p])
        kv[p] = got[0:64].astype(bf16)
        mean = rounded((got[64:65] + got[65:66] + got[66:67]) / total)
        tail[p:p + 1, :] = mean
        means[p] = mean
        return jnp.where(lane640 == 512 + p, jnp.log(total), bias)

    for p in range(4):
        bias = compact_page(p, bias)

    w1_wait(0, win_w.at[z])

    @pl.loop(1, 8)
    def _(j):
        z_copy(0, win_w, j).start()

    w1_wait(1, wo_w.at[z])

    @pl.loop(1, 8)
    def _(j):
        z_copy(1, wo_w, j).start()

    @pl.loop(1, 16)
    def _(j):
        gu_copy(j).start()

    w1_send(2)
    for p in range(4, 8):
        bias = compact_page(p, bias)

    pltpu.make_async_copy(gu_w.at[z, pl.ds(0, 15)], gu_w.at[z, pl.ds(0, 15)], r_ph.at[7]).wait()
    w1_wait(2, wd_w.at[z, :, pl.ds(0, 6)])
    ring_step(1)

    own_len = jnp.sum(
        jnp.where(holds(8, 2 * group), jnp.broadcast_to(lengths_ref[...].astype(f32), (8, 256)), 0.0),
        axis=1, keepdims=True,
    )[0:2]
    cos2 = jnp.zeros((2, 128), f32)
    sin2 = jnp.zeros((2, 128), f32)
    for k in range(NP):
        cos2 = jnp.where(own_len == k + 1.0, turn_ref[k:k + 1, :], cos2)
        sin2 = jnp.where(own_len == k + 1.0, turn_ref[NP + k:NP + k + 1, :], sin2)
    table = table_ref[...].astype(f32)
    entry = iota((2, 640), 1)
    page_of = jnp.where(entry < 512, entry >> 6, entry - 512).astype(f32)
    owned = jnp.zeros((2, 640), f32)
    for k in range(4):
        logical = 4 * k + x
        spot_of = jnp.sum(jnp.where(iota((2, NP), 1) == logical, table, 0.0), axis=1, keepdims=True)
        alive = jnp.where(own_len > logical.astype(f32), 1.0, 0.0)
        owned = jnp.where(page_of == spot_of, alive, owned)
    listed = jnp.concatenate(
        [keep_ref[k:k + 1, :] for k in range(8)] + [jnp.zeros((1, 128), i32)], axis=1
    )
    owned = jnp.where((entry < 520) & (listed >= 0), owned, 0.0)
    allow = jnp.where((entry == 520 + iota((2, 640), 0)) & (x == 0), 1.0, owned)

    sel_row = iota((512, 128), 0)
    sel_col = iota((512, 128), 1)
    select = (
        ((sel_row & 127) >> 5 == yb)
        & (sel_col >> 5 == sel_row >> 7)
        & ((sel_row & 31) == (sel_col & 31))
    ).astype(bf16)

    pltpu.make_async_copy(hx.at[pl.ds(0, 3)], hx.at[pl.ds(0, 3)], r_ph.at[0]).wait()
    square = jnp.zeros((32, 1), f32)
    for k in range(4):
        part = hx[k].astype(f32)
        square += jnp.sum(part * part, axis=1, keepdims=True)
    scale = lax.rsqrt(square * (1.0 / D) + epsilon)
    pieces = []
    for k in range(4):
        normed = (hx[k].astype(f32) * scale * again_ref[:, k * 512:(k + 1) * 512]).astype(bf16)
        pieces.append(dot(normed, select).astype(bf16))
    x_in = jnp.concatenate(pieces, axis=1)

    pltpu.make_async_copy(seven(win_w), seven(win_w), r_z.at[0]).wait()
    partial = dot(x_in, win_w[...].reshape(512, 128))
    for k in range(16):
        pb[k] = partial[2 * k:2 * k + 2, :]
    rb[yc] = pb[yc]

    def b_copy(j):
        return remote(pb.at[yc_peer(j)], rb.at[yc], s_ph.at[1], r_ph.at[1], dev(z, yc_peer(j), x))

    @pl.loop(1, 16)
    def _(j):
        b_copy(j).start()

    ring_step(2)
    fifteen = pl.ds(0, 15)
    pltpu.make_async_copy(rb.at[fifteen], rb.at[fifteen], r_ph.at[1]).wait()
    for a in range(4):
        cx[x, a] = rounded(rb[4 * a] + rb[4 * a + 1] + rb[4 * a + 2] + rb[4 * a + 3])

    def c_copy(j):
        return remote(cx.at[x], cx.at[x], s_ph.at[2], r_ph.at[2], dev(z, yc, x_peer(j)))

    for j in range(1, 4):
        c_copy(j).start()
    three = pl.ds(0, 3)
    pltpu.make_async_copy(cx.at[three], cx.at[three], r_ph.at[2]).wait()
    for k in range(16):
        fa[2 * k:2 * k + 2, :] = cx[k // 4, k % 4]

    mixed = fa[...]
    row = iota((32, 128), 0)
    lane = iota((32, 128), 1)
    low = lane < 64
    block = row >> 1
    moved = pltpu.roll(pltpu.roll(mixed, 30, 0), 64, 1)
    mixed = jnp.where(((block == 3) | (block == 11)) & ~low, mixed + moved, mixed)
    sq = mixed * mixed
    ms_low = jnp.sum(jnp.where(low, sq, 0.0), axis=1, keepdims=True) * (1.0 / HD)
    ms_high = jnp.sum(jnp.where(low, 0.0, sq), axis=1, keepdims=True) * (1.0 / HD)
    inverse = jnp.where(low, lax.rsqrt(ms_low + epsilon), lax.rsqrt(ms_high + epsilon))
    place = block * 2 + jnp.where(low, 0, 1)
    qgain = jnp.concatenate([qgain_ref[...]] * 2, axis=1)
    kgain = jnp.concatenate([kgain_ref[...]] * 2, axis=1)
    gain = jnp.where(place <= 20, qgain, kgain)
    vec = mixed * inverse * gain
    even_row = (row & 1) == 0
    cosine = jnp.where(even_row, cos2[0:1, :], cos2[1:2, :])
    sine = jnp.where(even_row, sin2[0:1, :], sin2[1:2, :])
    first_half = (lane & 63) < 32
    rotated = jnp.where(
        first_half,
        vec * cosine - pltpu.roll(vec, 96, 1) * sine,
        vec * cosine + pltpu.roll(vec, 32, 1) * sine,
    )
    final = jnp.where(place >= 27, mixed, rounded(rotated))
    swapped = pltpu.roll(final, 64, 1)
    low2 = low[0:2]

    def two(values, b):
        return values[2 * b:2 * b + 2, :]

    tail[8:10, 0:128] = jnp.where(low2, two(swapped, 10), two(swapped, 11))
    tail[8:10, 128:256] = jnp.where(low2, two(swapped, 11), two(final, 12))
    tail[8:10, 256:384] = two(final, 13)
    tail[8:10, 384:512] = two(final, 14)
    tail[8:10, 512:640] = two(final, 15)
    kv[8, 0:16] = tail[...].astype(bf16)
    kv[8, 16:64] = jnp.zeros((48, 640), bf16)
    kv[9] = jnp.zeros((64, 640), bf16)

    lowq = low[0:QROWS]
    fq = final[0:QROWS]
    gq = swapped[0:QROWS]
    both = jnp.concatenate([jnp.where(lowq, fq, gq), jnp.where(lowq, gq, fq)], axis=0)
    nrow = 2 * QROWS

    def row_facts(width):
        at = iota((nrow, width), 0)
        second = at >= QROWS
        inside = jnp.where(second, at - QROWS, at)
        request = inside & 1
        spot = (inside >> 1) * 2 + jnp.where(second, 1, 0)
        head = jnp.where(spot <= 7, spot, spot - 1)
        valid = (spot != 8) & (spot <= 20)
        return request, head, valid

    request, head, valid = row_facts(384)
    lane384 = iota((nrow, 384), 1)
    queries = jnp.where(
        valid & (lane384 >> 6 == head >> 2), jnp.concatenate([both, both, both], axis=1), 0.0
    ).astype(bf16)
    scores = dot_t(queries, kv[:, :, 0:384].reshape(640, 384)) * (HD ** (-0.5)) + bias
    request640, _, _ = row_facts(640)
    permit = jnp.where(request640 == 0, allow[0:1, :], allow[1:2, :]) > 0.5
    scores = jnp.where(permit, scores, negative)
    top = jnp.max(scores, axis=1, keepdims=True)
    weight = jnp.where(permit, jnp.exp(scores - top), 0.0)
    mass = jnp.sum(weight, axis=1, keepdims=True)
    w1 = rounded(weight)
    w2 = rounded(weight - w1)
    w3 = weight - w1 - w2
    summed = dot(jnp.concatenate([w1, w2, w3], axis=0).astype(bf16), kv[:, :, 256:640].reshape(640, 384))
    summed = summed[0:nrow] + summed[nrow:2 * nrow] + summed[2 * nrow:3 * nrow]
    summed = jnp.where(lane384 >> 6 == (head >> 2) + 1, summed, 0.0)
    folded = summed[:, 0:128] + summed[:, 128:256] + summed[:, 256:384]
    folded = folded + pltpu.roll(folded, 64, 1)
    lane128 = iota((nrow, 128), 1)
    dx[x] = jnp.where(
        lane128 < 64, folded, jnp.where(lane128 == 64, mass, jnp.where(lane128 == 65, top, 0.0))
    )

    def d_copy(j):
        return remote(dx.at[x], dx.at[x], s_ph.at[3], r_ph.at[3], dev(z, yc, x_peer(j)))

    for j in range(1, 4):
        d_copy(j).start()
    ring_step(3)

    for f in range(8):
        page = 0
        for q in range(1, 8):
            page = jnp.where(dest_ref[0, q] == f, q, page)
        compact_ref[f // 2, (f % 2) * 64:(f % 2) * 64 + 64, :] = kv[page]
        sumr[f:f + 1, :] = means[page]
    summary_ref[...] = sumr[...].astype(bf16)
    stores = [
        pltpu.make_async_copy(compact_ref, compact_hbm, s_out.at[0]),
        pltpu.make_async_copy(summary_ref, summary_hbm, s_out.at[1]),
        pltpu.make_async_copy(out_ref, out_hbm, s_out.at[2]),
    ]
    stores[0].start()
    stores[1].start()

    kap = iota((1, 2048), 1)
    kclass = kap >> 9
    kz = (kap >> 6) & 7
    kyh = (kap >> 5) & 1
    kc = (kap >> 4) & 1
    ki = kap & 15
    feature = 10 * (kz * 16 + (4 * kyh + kclass) * 2 + kc) + ki
    real = ki < 10
    spread = (((feature & 63) == iota((128, 2048), 0)) & real).astype(bf16)

    pltpu.make_async_copy(dx.at[three], dx.at[three], r_ph.at[3]).wait()
    parts = [dx[k] for k in range(4)]
    tops = [at_lane(part, 65) for part in parts]
    best = jnp.maximum(jnp.maximum(tops[0], tops[1]), jnp.maximum(tops[2], tops[3]))
    acc = jnp.zeros((nrow, 128), f32)
    for k in range(4):
        acc += parts[k] * jnp.exp(tops[k] - best)
    attention = jnp.where(lane128 < 64, acc / at_lane(acc, 64), 0.0).astype(bf16)
    _, head2048, valid2048 = row_facts(2048)
    spread_rows = dot(attention, spread)
    spread_rows = jnp.where(valid2048 & (head2048 == feature >> 6), spread_rows, 0.0).astype(bf16)
    pick_at = iota((8, nrow), 1)
    pick_second = jnp.where(pick_at >= QROWS, pick_at - QROWS, pick_at)
    pick = ((pick_second & 1) == iota((8, nrow), 0)).astype(bf16)
    grouped = dot(pick, spread_rows)
    for k in range(4):
        eb[k] = grouped[0:2, k * 512:(k + 1) * 512]
    ex[yc] = eb[yb]

    def e_copy(j):
        return remote(
            eb.at[lax.rem(yc_peer(j), 4)], ex.at[yc], s_ph.at[4], r_ph.at[4], dev(z, yc_peer(j), x)
        )

    @pl.loop(1, 16)
    def _(j):
        e_copy(j).start()

    ring_step(4)
    pltpu.make_async_copy(seven(wo_w), seven(wo_w), r_z.at[1]).wait()
    pltpu.make_async_copy(ex.at[fifteen], ex.at[fifteen], r_ph.at[4]).wait()
    for k in range(16):
        xa[2 * k:2 * k + 2, :] = ex[k]
    ox[yb] = dot(xa[...].astype(bf16), wo_w[...].reshape(512, 128))

    def o_copy(j):
        return remote(ox.at[yb], ox.at[yb], s_ph.at[5], r_ph.at[5], dev(z, ya * 4 + yb_peer(j), x))

    for j in range(1, 4):
        o_copy(j).start()
    pltpu.make_async_copy(ox.at[three], ox.at[three], r_ph.at[5]).wait()
    residual = jnp.zeros((32, 128), f32)
    own_rows = hx[x]
    for k in range(4):
        residual = jnp.where(ya == k, own_rows[:, k * 128:(k + 1) * 128].astype(f32), residual)
    mid = (residual + (ox[0] + ox[1] + ox[2] + ox[3])).astype(bf16)
    mx[col] = mid
    mid_f[...] = mid.astype(f32)

    def m_copy(buf, n, j):
        peer = col_peer(j)
        return remote(
            buf.at[col], buf.at[col], s_ph.at[n], r_ph.at[n], dev(z, lax.rem(peer, 4) * 4 + yb, peer // 4)
        )

    @pl.loop(1, 16)
    def _(j):
        m_copy(mx, 6, j).start()

    pltpu.make_async_copy(mx.at[fifteen], mx.at[fifteen], r_ph.at[6]).wait()
    square = jnp.zeros((32, 128), f32)
    for k in range(16):
        part = mx[k].astype(f32)
        square += part * part
    scale = lax.rsqrt(jnp.sum(square, axis=1, keepdims=True) * (1.0 / D) + epsilon)
    tiles = []
    for k in range(16):
        tiles.append((mx[k].astype(f32) * scale * fgain_ref[:, k * 128:(k + 1) * 128]).astype(bf16))
    x_mid = jnp.concatenate(tiles, axis=1)

    ring_step(5)
    sums = dot(x_mid, gu_w[...].reshape(2048, 256))
    gate_sum = sums[:, 0:128]
    ax[col] = (gate_sum / (1.0 + jnp.exp(-gate_sum)) * sums[:, 128:256]).astype(bf16)

    @pl.loop(1, 16)
    def _(j):
        m_copy(ax, 8, j).start()

    pltpu.make_async_copy(ax.at[fifteen], ax.at[fifteen], r_ph.at[8]).wait()
    whole = jnp.concatenate([ax[k] for k in range(16)], axis=1)
    down = dot(whole, wd_w[...].reshape(2048, 128))
    for k in range(4):
        ys[k] = down[8 * k:8 * k + 8, :]
    yx[yb] = ys[yb]

    def y_copy(j):
        return remote(ys.at[yb_peer(j)], yx.at[yb], s_ph.at[9], r_ph.at[9], dev(z, ya * 4 + yb_peer(j), x))

    for j in range(1, 4):
        y_copy(j).start()
    pltpu.make_async_copy(yx.at[three], yx.at[three], r_ph.at[9]).wait()
    mine = mid_f[pl.ds(pl.multiple_of(yb * 8, 8), 8), :]
    outer = jnp.where(c == 0, y, z)
    inner = jnp.where(c == 0, z, y)
    jx[c, outer, inner] = (mine + (yx[0] + yx[1] + yx[2] + yx[3])).astype(bf16)

    def along(value, first):
        zz = jnp.where((c == 0) == first, value, z)
        yy = jnp.where((c == 0) == first, y, value)
        return dev(zz, yy * 2 + c, x)

    mate = dev(z, y * 2 + 1 - c, x)

    @pl.loop(1, 8)
    def _(j):
        block = jx.at[c, outer, inner]
        remote(block, block, s_ph.at[10], r_ph.at[10], along(lax.rem(inner + j, 8), True)).start()

    pltpu.make_async_copy(jx.at[0, 0, pl.ds(0, 7)], jx.at[0, 0, pl.ds(0, 7)], r_ph.at[10]).wait()

    def j_copy(j):
        block = jx.at[c, outer]
        return remote(block, block, s_ph.at[11], r_j.at[outer], along(lax.rem(outer + j, 8), False))

    def m_forward(at):
        block = jx.at[c, at]
        return remote(block, block, s_ph.at[12], r_ph.at[12], mate)

    @pl.loop(1, 8)
    def _(j):
        j_copy(j).start()

    m_forward(outer).start()

    into = (iota((256, 128), 0) >> 1 == iota((256, 128), 1)).astype(bf16)
    group_of = dot_t(into, jnp.broadcast_to(source, (8, 128)).astype(bf16))[:, 0:1]
    request_id = iota((256, 256), 0)
    spot = iota((256, 256), 1)
    held_row = ((spot >> 3) & 7) * 32 + (spot >> 7) * 16 + ((spot >> 6) & 1) * 8 + (spot & 7)
    wanted = jnp.where((request_id & 1) == 0, request_id.astype(f32), 2.0 * group_of + 1.0)
    back = (held_row.astype(f32) == wanted).astype(bf16)

    @pl.loop(1, 8)
    def _(j):
        at = lax.rem(outer + 8 - j, 8)
        block = jx.at[c, at]
        remote(block, block, s_ph.at[11], r_j.at[at], mate).wait_recv()
        m_forward(at).start()

    pltpu.make_async_copy(jx.at[0], jx.at[0], r_ph.at[12]).wait()
    for a in range(4):
        blocks = []
        for h in range(2):
            blocks.append(jx[0, 2 * a + h].reshape(64, 128))
            blocks.append(jx[1, :, 2 * a + h].reshape(64, 128))
        out_ref[:, a * 128:(a + 1) * 128] = dot(back, jnp.concatenate(blocks, axis=0)).astype(bf16)

    stores[2].start()


    def sent(block, sem):
        pltpu.make_async_copy(block, block, sem).wait()

    for m in range(3):
        for a in range(4):
            src, dst, which = w1_parts(a)[m]
            target = a * 4 + cls

            @pl.when(target != yc)
            def _():
                remote(src, dst, s_w1.at[which, a], r_w1.at[which], dev(z, target, x)).wait_send()

    sent(seven(win_w), s_z.at[0])
    sent(seven(wo_w), s_z.at[1])
    for step in range(1, 5):
        for which in range(2):
            for way in ways(step):
                ring(step, way, which).wait_send()
    sent(hx.at[three], s_ph.at[0])
    sent(rb.at[fifteen], s_ph.at[1])
    sent(cx.at[three], s_ph.at[2])
    sent(dx.at[three], s_ph.at[3])
    sent(ex.at[fifteen], s_ph.at[4])
    sent(ox.at[three], s_ph.at[5])
    sent(mx.at[fifteen], s_ph.at[6])
    sent(gu_w.at[z, pl.ds(0, 15)], s_ph.at[7])
    sent(ax.at[fifteen], s_ph.at[8])
    sent(yx.at[three], s_ph.at[9])
    sent(jx.at[0, 0, pl.ds(0, 7)], s_ph.at[10])
    sent(jx.at[0, pl.ds(0, 7)], s_ph.at[11])
    sent(jx.at[0], s_ph.at[12])
    for store in stores:
        store.wait()


def hand_over(a_ref, b_ref, c_ref, a_out, b_out, c_out, sem):
    copies = [
        pltpu.make_async_copy(src, dst, sem.at[k])
        for k, (src, dst) in enumerate(((a_ref, a_out), (b_ref, b_out), (c_ref, c_out)))
    ]
    for copy in copies:
        copy.start()
    for copy in copies:
        copy.wait()


def rotation_table():
    half = HD // 2
    frequency = np.float32(10000.0) ** (-np.arange(half, dtype=np.float32) / np.float32(half))
    positions = (PAGE * np.arange(1, NP + 1)).astype(np.float32)
    angles = np.tile((positions[:, None] * frequency[None, :]).astype(np.float64), (1, 4))
    return np.concatenate([np.cos(angles), np.sin(angles)], axis=0).astype(np.float32)


def on_device(
    hidden_in, attention_gain, query_gain, key_gain, feedforward_gain,
    input_weight, output_weight, gate_weight, up_weight, down_weight,
    old_cache, keep_rows, drop_weights, dest_slots, lengths, page_table, source,
):
    operands = (
        hidden_in, input_weight, output_weight, gate_weight, up_weight, down_weight,
        old_cache, keep_rows, drop_weights, dest_slots,
        lengths[None, :], page_table, source[None, :],
        attention_gain[None, :], feedforward_gain[None, :], query_gain[None, :], key_gain[None, :],
        jnp.asarray(rotation_table()),
    )
    hbm = pl.BlockSpec(memory_space=pltpu.HBM)
    dma = pltpu.SemaphoreType.DMA

    def scratch(*shape, dtype=f32):
        return pltpu.VMEM(shape, dtype)

    results = pl.pallas_call(
        kernel,
        name="decode",
        out_shape=(
            jax.ShapeDtypeStruct((4, PAGE, KVW), bf16),
            jax.ShapeDtypeStruct((8, KVW), bf16),
            jax.ShapeDtypeStruct(hidden_in.shape, bf16),
        ),
        in_specs=[hbm] * len(operands),
        out_specs=(hbm, hbm, hbm),
        scratch_shapes=[
            (pltpu.SMEM if k == 9 else pltpu.VMEM)(a.shape, a.dtype) for k, a in enumerate(operands)
        ] + [
            scratch(4, 32, 512, dtype=bf16),
            scratch(4, 16, 128, dtype=bf16),
            scratch(4, 16, 128, dtype=bf16),
            scratch(16, 16, 256, dtype=bf16),
            scratch(4, 3, 16, 128, dtype=bf16),
            scratch(8, 4, 16, 128, dtype=bf16),
            scratch(8, 4, 16, 128, dtype=bf16),
            scratch(8, 16, 16, 256, dtype=bf16),
            scratch(8, 2, 8, 16, 128, dtype=bf16),
            scratch(16, 2, 128),
            scratch(16, 2, 128),
            scratch(4, 4, 2, 128),
            scratch(32, 128),
            scratch(10, 64, 640, dtype=bf16),
            scratch(16, 640),
            scratch(4, 2 * QROWS, 128),
            scratch(4, 2, 512),
            scratch(16, 2, 512),
            scratch(32, 512),
            scratch(4, 32, 128),
            scratch(16, 32, 128, dtype=bf16),
            scratch(32, 128),
            scratch(16, 32, 128, dtype=bf16),
            scratch(4, 8, 128),
            scratch(4, 8, 128),
            scratch(2, 8, 8, 8, 128, dtype=bf16),
            scratch(8, 640),
            scratch(8, 1, 640),
            scratch(4, PAGE, KVW, dtype=bf16),
            scratch(8, KVW, dtype=bf16),
            scratch(*hidden_in.shape, dtype=bf16),
            dma((len(operands),)), dma((3,)),
            dma((3, 4)), dma((3,)),
            dma((2,)), dma((2,)),
            dma((2, 4, 2)), dma((2, 4, 2)),
            dma((13,)), dma((13,)), dma((8,)),
        ],
        compiler_params=pltpu.CompilerParams(
            collective_id=0, has_side_effects=True, vmem_limit_bytes=63 << 20
        ),
    )(*operands)
    return pl.pallas_call(
        hand_over,
        name="hand_over",
        out_shape=tuple(jax.ShapeDtypeStruct(a.shape, a.dtype) for a in results),
        in_specs=[hbm] * 3,
        out_specs=(pl.BlockSpec(memory_space=pltpu.VMEM),) * 3,
        scratch_shapes=[dma((3,))],
    )(*results)


def solution(mesh):
    placed = (
        P(None, "head"),
        P(),
        P(),
        P(),
        P(),
        P("req", "head"),
        P("req", "head"),
        P("req", "head"),
        P("req", "head"),
        P("req", "head"),
        P(("req", "head"), None, None),
        P(("req", "head"), None),
        P(("req", "head"), None),
        P(("req", "head"), None),
        P(),
        P("req", None),
        P(),
    )
    return jax.shard_map(
        on_device,
        mesh=mesh,
        in_specs=placed,
        out_specs=(P(("req", "head"), None, None), P(("req", "head"), None), P(None, "head")),
        check_vma=False,
    )
```

```python
import jax
import jax.numpy as jnp
import numpy as np
from jax import lax
from jax.experimental import pallas as pl
from jax.experimental.pallas import tpu as pltpu
from jax.sharding import PartitionSpec as P

D = 2048
HEADS = 20
KVH = 5
HD = 64
PAGE = 128
KEEP = 64
NP = 16
R_DEV = 2
KVW = 640
QROWS = 24

epsilon = 1e-06
negative = -1e30
bf16 = jnp.bfloat16
f32 = jnp.float32
i32 = jnp.int32


def iota(shape, dim):
    return lax.broadcasted_iota(i32, shape, dim)


def dot(a, b):
    return jnp.dot(a, b, preferred_element_type=f32)


def dot_t(a, b):
    return lax.dot_general(a, b, (((1,), (1,)), ((), ())), preferred_element_type=f32)


def rounded(values):
    return values.astype(bf16).astype(f32)


def at_lane(values, lane):
    return jnp.sum(jnp.where(iota(values.shape, 1) == lane, values, 0.0), axis=1, keepdims=True)


def kernel(
    hidden_hbm, win_hbm, wo_hbm, wg_hbm, wu_hbm, wd_hbm, cache_hbm, keep_hbm, drop_hbm, dest_hbm,
    lengths_hbm, table_hbm, source_hbm, again_hbm, fgain_hbm, qgain_hbm, kgain_hbm, turn_hbm,
    compact_hbm, summary_hbm, out_hbm,
    hidden_ref, win_ref, wo_ref, wg_ref, wu_ref, wd_ref, cache_ref, keep_ref, drop_ref, dest_ref,
    lengths_ref, table_ref, source_ref, again_ref, fgain_ref, qgain_ref, kgain_ref, turn_ref,
    hx, wo_s, gu_s, wd_s, win_w, wo_w, gu_w, wd_w,
    pb, rb, cx, fa, kv, tail, dx, eb, ex, xa, ox, mx, mid_f, ax, ys, yx, jx, sumr, means, compact_ref, summary_ref, out_ref,
    s_in, s_out, s_w1, r_w1, s_z, r_z, s_ring, r_ring, s_ph, r_ph, r_j,
):
    loads = [
        pltpu.make_async_copy(src, dst, s_in.at[k])
        for k, (src, dst) in enumerate((
            (win_hbm, win_ref), (source_hbm, source_ref), (hidden_hbm, hidden_ref), (wo_hbm, wo_ref),
            (wg_hbm, wg_ref), (wu_hbm, wu_ref), (wd_hbm, wd_ref), (keep_hbm, keep_ref),
            (drop_hbm, drop_ref), (cache_hbm, cache_ref), (dest_hbm, dest_ref), (lengths_hbm, lengths_ref),
            (table_hbm, table_ref), (again_hbm, again_ref), (fgain_hbm, fgain_ref), (qgain_hbm, qgain_ref),
            (kgain_hbm, kgain_ref), (turn_hbm, turn_ref),
        ))
    ]
    for load in loads:
        load.start()
    group = lax.axis_index("req")
    x = lax.axis_index("head")
    z = group // 16
    yc = lax.rem(group, 16)
    ya = yc // 4
    yb = lax.rem(yc, 4)
    y = yc // 2
    c = lax.rem(yc, 2)
    col = x * 4 + ya

    def dev(zz, yy, xx):
        return {"req": zz * 16 + yy, "head": xx}

    def remote(src, dst, ssem, rsem, target):
        return pltpu.make_async_remote_copy(
            src_ref=src, dst_ref=dst, send_sem=ssem, recv_sem=rsem,
            device_id=target, device_id_type=pl.DeviceIdType.MESH,
        )

    def yc_peer(j):
        return lax.rem(yc + j, 16)

    def col_peer(j):
        return lax.rem(col + j, 16)

    def x_peer(j):
        return lax.rem(x + j, 4)

    def yb_peer(j):
        return lax.rem(yb + j, 4)

    def z_peer(j):
        return lax.rem(z + j, 8)

    wd_w[:, :, 6:8] = jnp.zeros((8, 2, 2, 16, 128), bf16)

    barrier = pltpu.get_barrier_semaphore()

    def greet(target):
        pl.semaphore_signal(barrier, inc=1, device_id=target, device_id_type=pl.DeviceIdType.MESH)

    @pl.loop(1, 16)
    def _(j):
        greet(dev(z, yc_peer(j), x))

    for j in range(1, 4):
        greet(dev(z, yc, x_peer(j)))

    @pl.loop(1, 8)
    def _(j):
        greet(dev(z_peer(j), yc, x))

    for k in range(2):
        loads[k].wait()
    win = win_ref[...]
    pad = jnp.zeros((16, 32), bf16)
    even = jnp.concatenate([win, pad], axis=1)
    odd = jnp.concatenate([pad, win], axis=1)
    shifted = jnp.where(lax.rem(x, 2) == 0, even, odd)
    win_w[z] = shifted

    source = source_ref[...].astype(f32)
    doubling = (iota((128, 256), 1) >> 1 == iota((128, 256), 0)).astype(bf16)
    source_of = dot(jnp.broadcast_to(source, (8, 128)).astype(bf16), doubling)

    def holds(rows, first):
        at = iota((rows, 256), 0)
        request = iota((rows, 256), 1)
        plain = ((at & 1) == 0) & (request == first + at)
        origin = jnp.broadcast_to(source_of[0:1], (rows, 256))
        carried = ((at & 1) == 1) & ((request & 1) == 1) & (origin == ((first + at) >> 1).astype(f32))
        return plain | carried

    chosen = jnp.where(holds(32, 32 * z), 1.0, 0.0).astype(bf16)
    loads[2].wait()
    hx[x] = dot(chosen, hidden_ref[...]).astype(bf16)

    pl.semaphore_wait(barrier, 25)

    def h_copy(j):
        return remote(hx.at[x], hx.at[x], s_ph.at[0], r_ph.at[0], dev(z, yc, x_peer(j)))

    cls = lax.rem(y, 4)
    yh = y // 4
    slot = yh * 2 + c

    def w1_parts(a):
        return (
            (wo_s.at[a], wo_w.at[z, slot], 0),
            (wd_s.at[a], wd_w.at[z, yh, pl.ds(c * 3, 3)], 1),
        )

    def w1_send(m):
        for a in range(4):
            src, dst, which = w1_parts(a)[m]
            target = a * 4 + cls

            @pl.when(target != yc)
            def _():
                remote(src, dst, s_w1.at[which, a], r_w1.at[which], dev(z, target, x)).start()

            @pl.when(target == yc)
            def _():
                pltpu.make_async_copy(src, dst, r_w1.at[which]).start()

    def w1_wait(which, block):
        pltpu.make_async_copy(block, block, r_w1.at[which]).wait()

    def z_copy(which, buf, j):
        return remote(buf.at[z], buf.at[z], s_z.at[which], r_z.at[which], dev(z_peer(j), yc, x))

    def seven(buf):
        return buf.at[pl.ds(0, 7)]

    @pl.loop(1, 8)
    def _(j):
        z_copy(0, win_w, j).start()

    for j in range(1, 4):
        h_copy(j).start()

    for k in range(3, 7):
        loads[k].wait()
    wo_full = jnp.concatenate([wo_ref[...], jnp.zeros((6, 512), bf16)], axis=0)
    wd_full = jnp.concatenate([wd_ref[...], jnp.zeros((8, 512), bf16)], axis=0)
    gu_s[...] = jnp.zeros_like(gu_s)
    gate = wg_ref[...]
    up = wu_ref[...]
    for a in range(4):
        lanes = slice(a * 128, (a + 1) * 128)
        wo_s[a] = wo_full[:, lanes]
        for k in range(3):
            wd_s[a, k] = wd_full[k * 16:(k + 1) * 16, lanes]
        for k in range(4):
            for h in range(2):
                first = a * 320 + k * 80 + h * 40
                gu_s[a * 4 + k, :, h * 48:h * 48 + 40] = gate[:, first:first + 40]
                gu_s[a * 4 + k, :, 128 + h * 48:128 + h * 48 + 40] = up[:, first:first + 40]
    w1_send(0)
    gu_w[z, yc] = gu_s[yc]

    def gu_copy(j):
        return remote(gu_s.at[yc_peer(j)], gu_w.at[z, yc], s_ph.at[7], r_ph.at[7], dev(z, yc_peer(j), x))


    @pl.loop(1, 16)
    def _(j):
        gu_copy(j).start()

    def ring(step, way, which):
        block = lax.rem(z - (step - 1) + 8, 8) if way == 0 else lax.rem(z + step - 1, 8)
        target = lax.rem(z + 1, 8) if way == 0 else lax.rem(z + 7, 8)
        ref = gu_w.at[block] if which == 0 else wd_w.at[block, :, pl.ds(0, 6)]
        return remote(ref, ref, s_ring.at[way, step - 1, which], r_ring.at[way, step - 1, which], dev(target, yc, x))

    def ways(step):
        return (0, 1) if step < 4 else (0,)

    def ring_step(step):
        for which in range(2):
            for way in (0, 1):
                if step > 1 and way in ways(step - 1):
                    ring(step - 1, way, which).wait_recv()
            if step <= 4:
                for way in ways(step):
                    ring(step, way, which).start()

    for k in range(7, 18):
        loads[k].wait()
    bias = jnp.zeros((1, 640), f32)
    tail[...] = jnp.zeros_like(tail)
    lane640 = iota((1, 640), 1)
    row_ids = iota((64, 128), 1).astype(f32)
    eye = (iota((64, 64), 0) == iota((64, 64), 1)).astype(bf16)
    keep_all = dot_t(eye, keep_ref[...].astype(f32).astype(bf16))

    def compact_page(p, bias):
        picks = (keep_all[:, p:p + 1] == row_ids).astype(f32)
        weight = drop_ref[p:p + 1, :] * (1.0 - jnp.sum(picks, axis=0, keepdims=True))
        total = jnp.sum(weight, axis=1, keepdims=True)
        w1 = rounded(weight)
        w2 = rounded(weight - w1)
        w3 = weight - w1 - w2
        left = jnp.concatenate([picks, w1, w2, w3, jnp.zeros((13, 128), f32)], axis=0).astype(bf16)
        got = dot(left, cache_ref[p])
        kv[p] = got[0:64].astype(bf16)
        mean = rounded((got[64:65] + got[65:66] + got[66:67]) / total)
        tail[p:p + 1, :] = mean
        means[p] = mean
        return jnp.where(lane640 == 512 + p, jnp.log(total), bias)

    for p in range(4):
        bias = compact_page(p, bias)

    w1_wait(0, wo_w.at[z])

    @pl.loop(1, 8)
    def _(j):
        z_copy(1, wo_w, j).start()

    w1_send(1)
    pltpu.make_async_copy(gu_w.at[z, pl.ds(0, 15)], gu_w.at[z, pl.ds(0, 15)], r_ph.at[7]).wait()
    w1_wait(1, wd_w.at[z, :, pl.ds(0, 6)])
    ring_step(1)

    for p in range(4, 8):
        bias = compact_page(p, bias)

    own_len = jnp.sum(
        jnp.where(holds(8, 2 * group), jnp.broadcast_to(lengths_ref[...].astype(f32), (8, 256)), 0.0),
        axis=1, keepdims=True,
    )[0:2]
    cos2 = jnp.zeros((2, 128), f32)
    sin2 = jnp.zeros((2, 128), f32)
    for k in range(NP):
        cos2 = jnp.where(own_len == k + 1.0, turn_ref[k:k + 1, :], cos2)
        sin2 = jnp.where(own_len == k + 1.0, turn_ref[NP + k:NP + k + 1, :], sin2)
    table = table_ref[...].astype(f32)
    entry = iota((2, 640), 1)
    page_of = jnp.where(entry < 512, entry >> 6, entry - 512).astype(f32)
    owned = jnp.zeros((2, 640), f32)
    for k in range(4):
        logical = 4 * k + x
        spot_of = jnp.sum(jnp.where(iota((2, NP), 1) == logical, table, 0.0), axis=1, keepdims=True)
        alive = jnp.where(own_len > logical.astype(f32), 1.0, 0.0)
        owned = jnp.where(page_of == spot_of, alive, owned)
    listed = jnp.concatenate(
        [keep_ref[k:k + 1, :] for k in range(8)] + [jnp.zeros((1, 128), i32)], axis=1
    )
    owned = jnp.where((entry < 520) & (listed >= 0), owned, 0.0)
    allow = jnp.where((entry == 520 + iota((2, 640), 0)) & (x == 0), 1.0, owned)

    sel_row = iota((512, 128), 0)
    sel_col = iota((512, 128), 1)
    match = (
        (sel_row >> 8 == (sel_col >> 4) & 1)
        & ((sel_row >> 4) & 15 == yc)
        & ((sel_row & 15) == (sel_col & 15))
    )
    selects = [(match & (sel_col >> 5 == k)).astype(bf16) for k in range(4)]

    pltpu.make_async_copy(hx.at[pl.ds(0, 3)], hx.at[pl.ds(0, 3)], r_ph.at[0]).wait()
    square = jnp.zeros((32, 1), f32)
    for k in range(4):
        part = hx[k].astype(f32)
        square += jnp.sum(part * part, axis=1, keepdims=True)
    scale = lax.rsqrt(square * (1.0 / D) + epsilon)
    x_in = jnp.zeros((32, 128), f32)
    for k in range(4):
        normed = (hx[k].astype(f32) * scale * again_ref[:, k * 512:(k + 1) * 512]).astype(bf16)
        x_in += dot(normed, selects[k])

    pltpu.make_async_copy(seven(win_w), seven(win_w), r_z.at[0]).wait()
    partial = dot(x_in.astype(bf16), win_w[...].reshape(128, 512))
    for k in range(16):
        pb[k] = partial[2 * k:2 * k + 2, :]
    rb[yc] = pb[yc]

    def b_copy(j):
        return remote(pb.at[yc_peer(j)], rb.at[yc], s_ph.at[1], r_ph.at[1], dev(z, yc_peer(j), x))

    @pl.loop(1, 16)
    def _(j):
        b_copy(j).start()

    ring_step(2)
    fifteen = pl.ds(0, 15)
    pltpu.make_async_copy(rb.at[fifteen], rb.at[fifteen], r_ph.at[1]).wait()
    whole_qkv = rb[0]
    for k in range(1, 16):
        whole_qkv += rb[k]
    whole_qkv = rounded(whole_qkv)
    for a in range(4):
        cx[x, a] = whole_qkv[:, a * 128:(a + 1) * 128]

    def c_copy(j):
        return remote(cx.at[x], cx.at[x], s_ph.at[2], r_ph.at[2], dev(z, yc, x_peer(j)))

    for j in range(1, 4):
        c_copy(j).start()
    three = pl.ds(0, 3)
    row = iota((32, 128), 0)
    lane = iota((32, 128), 1)
    low = lane < 64
    block = row >> 1
    joins = ((block == 3) | (block == 11)) & ~low
    place = block * 2 + jnp.where(low, 0, 1)
    qgain = jnp.concatenate([qgain_ref[...]] * 2, axis=1)
    kgain = jnp.concatenate([kgain_ref[...]] * 2, axis=1)
    gain = jnp.where(place <= 20, qgain, kgain)
    even_row = (row & 1) == 0
    cosine = jnp.where(even_row, cos2[0:1, :], cos2[1:2, :])
    sine = jnp.where(even_row, sin2[0:1, :], sin2[1:2, :])
    sine = jnp.where((lane & 63) < 32, -sine, sine)
    nrow = 2 * QROWS

    def row_facts(width):
        at = iota((nrow, width), 0)
        second = at >= QROWS
        inside = jnp.where(second, at - QROWS, at)
        request = inside & 1
        spot = (inside >> 1) * 2 + jnp.where(second, 1, 0)
        head = jnp.where(spot <= 7, spot, spot - 1)
        valid = (spot != 8) & (spot <= 20)
        return request, head, valid

    request, head, valid = row_facts(384)
    lane384 = iota((nrow, 384), 1)
    asks = valid & (lane384 >> 6 == head >> 2)
    gets = lane384 >> 6 == (head >> 2) + 1
    request640, _, _ = row_facts(640)
    permit = jnp.where(request640 == 0, allow[0:1, :], allow[1:2, :]) > 0.5
    lane128 = iota((nrow, 128), 1)
    kv[9] = jnp.zeros((64, 640), bf16)
    kv[8, 16:64] = jnp.zeros((48, 640), bf16)

    pltpu.make_async_copy(cx.at[three], cx.at[three], r_ph.at[2]).wait()
    for k in range(16):
        fa[2 * k:2 * k + 2, :] = cx[k // 4, k % 4]

    mixed = fa[...]
    moved = pltpu.roll(pltpu.roll(mixed, 30, 0), 64, 1)
    mixed = jnp.where(joins, mixed + moved, mixed)
    sq = mixed * mixed
    ms_low = jnp.sum(jnp.where(low, sq, 0.0), axis=1, keepdims=True) * (1.0 / HD)
    ms_high = jnp.sum(jnp.where(low, 0.0, sq), axis=1, keepdims=True) * (1.0 / HD)
    inverse = jnp.where(low, lax.rsqrt(ms_low + epsilon), lax.rsqrt(ms_high + epsilon))
    vec = mixed * inverse * gain
    partner = jnp.where((lane & 63) < 32, pltpu.roll(vec, 96, 1), pltpu.roll(vec, 32, 1))
    rotated = vec * cosine + partner * sine
    final = jnp.where(place >= 27, mixed, rounded(rotated))
    swapped = pltpu.roll(final, 64, 1)
    low2 = low[0:2]

    def two(values, b):
        return values[2 * b:2 * b + 2, :]

    tail[8:10, 0:128] = jnp.where(low2, two(swapped, 10), two(swapped, 11))
    tail[8:10, 128:256] = jnp.where(low2, two(swapped, 11), two(final, 12))
    tail[8:10, 256:384] = two(final, 13)
    tail[8:10, 384:512] = two(final, 14)
    tail[8:10, 512:640] = two(final, 15)
    kv[8, 0:16] = tail[...].astype(bf16)

    lowq = low[0:QROWS]
    fq = final[0:QROWS]
    gq = swapped[0:QROWS]
    both = jnp.concatenate([jnp.where(lowq, fq, gq), jnp.where(lowq, gq, fq)], axis=0)
    queries = jnp.where(
        asks, jnp.concatenate([both, both, both], axis=1), 0.0
    ).astype(bf16)
    scores = dot_t(queries, kv[:, :, 0:384].reshape(640, 384)) * (HD ** (-0.5)) + bias
    scores = jnp.where(permit, scores, negative)
    top = jnp.max(scores, axis=1, keepdims=True)
    weight = jnp.where(permit, jnp.exp(scores - top), 0.0)
    mass = jnp.sum(weight, axis=1, keepdims=True)
    w1 = rounded(weight)
    w2 = rounded(weight - w1)
    w3 = weight - w1 - w2
    summed = dot(jnp.concatenate([w1, w2, w3], axis=0).astype(bf16), kv[:, :, 256:640].reshape(640, 384))
    summed = summed[0:nrow] + summed[nrow:2 * nrow] + summed[2 * nrow:3 * nrow]
    summed = jnp.where(gets, summed, 0.0)
    folded = summed[:, 0:128] + summed[:, 128:256] + summed[:, 256:384]
    folded = folded + pltpu.roll(folded, 64, 1)
    dx[x] = jnp.where(
        lane128 < 64, folded, jnp.where(lane128 == 64, mass, jnp.where(lane128 == 65, top, 0.0))
    )

    def d_copy(j):
        return remote(dx.at[x], dx.at[x], s_ph.at[3], r_ph.at[3], dev(z, yc, x_peer(j)))

    for j in range(1, 4):
        d_copy(j).start()
    ring_step(3)

    for f in range(8):
        page = 0
        for q in range(1, 8):
            page = jnp.where(dest_ref[0, q] == f, q, page)
        compact_ref[f // 2, (f % 2) * 64:(f % 2) * 64 + 64, :] = kv[page]
        sumr[f:f + 1, :] = means[page]
    summary_ref[...] = sumr[...].astype(bf16)
    stores = [
        pltpu.make_async_copy(compact_ref, compact_hbm, s_out.at[0]),
        pltpu.make_async_copy(summary_ref, summary_hbm, s_out.at[1]),
        pltpu.make_async_copy(out_ref, out_hbm, s_out.at[2]),
    ]
    stores[0].start()
    stores[1].start()

    kap = iota((1, 2048), 1)
    kclass = kap >> 9
    kz = (kap >> 6) & 7
    kyh = (kap >> 5) & 1
    kc = (kap >> 4) & 1
    ki = kap & 15
    feature = 10 * (kz * 16 + (4 * kyh + kclass) * 2 + kc) + ki
    real = ki < 10
    spread = (((feature & 63) == iota((128, 2048), 0)) & real).astype(bf16)

    _, head2048, valid2048 = row_facts(2048)
    belongs = valid2048 & (head2048 == feature >> 6)
    pick_at = iota((8, nrow), 1)
    pick_second = jnp.where(pick_at >= QROWS, pick_at - QROWS, pick_at)
    pick = ((pick_second & 1) == iota((8, nrow), 0)).astype(bf16)
    pltpu.make_async_copy(dx.at[three], dx.at[three], r_ph.at[3]).wait()
    parts = [dx[k] for k in range(4)]
    tops = [at_lane(part, 65) for part in parts]
    best = jnp.maximum(jnp.maximum(tops[0], tops[1]), jnp.maximum(tops[2], tops[3]))
    acc = jnp.zeros((nrow, 128), f32)
    for k in range(4):
        acc += parts[k] * jnp.exp(tops[k] - best)
    attention = jnp.where(lane128 < 64, acc / at_lane(acc, 64), 0.0).astype(bf16)
    spread_rows = dot(attention, spread)
    spread_rows = jnp.where(belongs, spread_rows, 0.0).astype(bf16)
    grouped = dot(pick, spread_rows)
    for k in range(4):
        eb[k] = grouped[0:2, k * 512:(k + 1) * 512]
    ex[yc] = eb[yb]

    def e_copy(j):
        return remote(
            eb.at[lax.rem(yc_peer(j), 4)], ex.at[yc], s_ph.at[4], r_ph.at[4], dev(z, yc_peer(j), x)
        )

    @pl.loop(1, 16)
    def _(j):
        e_copy(j).start()

    ring_step(4)
    pltpu.make_async_copy(seven(wo_w), seven(wo_w), r_z.at[1]).wait()
    pltpu.make_async_copy(ex.at[fifteen], ex.at[fifteen], r_ph.at[4]).wait()
    for k in range(16):
        xa[2 * k:2 * k + 2, :] = ex[k]
    ox[yb] = dot(xa[...].astype(bf16), wo_w[...].reshape(512, 128))

    def o_copy(j):
        return remote(ox.at[yb], ox.at[yb], s_ph.at[5], r_ph.at[5], dev(z, ya * 4 + yb_peer(j), x))

    for j in range(1, 4):
        o_copy(j).start()
    pltpu.make_async_copy(ox.at[three], ox.at[three], r_ph.at[5]).wait()
    residual = jnp.zeros((32, 128), f32)
    own_rows = hx[x]
    for k in range(4):
        residual = jnp.where(ya == k, own_rows[:, k * 128:(k + 1) * 128].astype(f32), residual)
    mid = (residual + (ox[0] + ox[1] + ox[2] + ox[3])).astype(bf16)
    mx[col] = mid
    mid_f[...] = mid.astype(f32)

    def m_copy(buf, n, j):
        peer = col_peer(j)
        return remote(
            buf.at[col], buf.at[col], s_ph.at[n], r_ph.at[n], dev(z, lax.rem(peer, 4) * 4 + yb, peer // 4)
        )

    @pl.loop(1, 16)
    def _(j):
        m_copy(mx, 6, j).start()

    pltpu.make_async_copy(mx.at[fifteen], mx.at[fifteen], r_ph.at[6]).wait()
    square = jnp.zeros((32, 128), f32)
    for k in range(16):
        part = mx[k].astype(f32)
        square += part * part
    scale = lax.rsqrt(jnp.sum(square, axis=1, keepdims=True) * (1.0 / D) + epsilon)
    tiles = []
    for k in range(16):
        tiles.append((mx[k].astype(f32) * scale * fgain_ref[:, k * 128:(k + 1) * 128]).astype(bf16))
    x_mid = jnp.concatenate(tiles, axis=1)

    ring_step(5)
    sums = dot(x_mid, gu_w[...].reshape(2048, 256))
    gate_sum = sums[:, 0:128]
    ax[col] = (gate_sum / (1.0 + jnp.exp(-gate_sum)) * sums[:, 128:256]).astype(bf16)

    @pl.loop(1, 16)
    def _(j):
        m_copy(ax, 8, j).start()

    pltpu.make_async_copy(ax.at[fifteen], ax.at[fifteen], r_ph.at[8]).wait()
    whole = jnp.concatenate([ax[k] for k in range(16)], axis=1)
    down = dot(whole, wd_w[...].reshape(2048, 128))
    for k in range(4):
        ys[k] = down[8 * k:8 * k + 8, :]
    yx[yb] = ys[yb]

    def y_copy(j):
        return remote(ys.at[yb_peer(j)], yx.at[yb], s_ph.at[9], r_ph.at[9], dev(z, ya * 4 + yb_peer(j), x))

    for j in range(1, 4):
        y_copy(j).start()
    pltpu.make_async_copy(yx.at[three], yx.at[three], r_ph.at[9]).wait()
    mine = mid_f[pl.ds(pl.multiple_of(yb * 8, 8), 8), :]
    outer = jnp.where(c == 0, y, z)
    inner = jnp.where(c == 0, z, y)
    jx[c, outer, inner] = (mine + (yx[0] + yx[1] + yx[2] + yx[3])).astype(bf16)

    def along(value, first):
        zz = jnp.where((c == 0) == first, value, z)
        yy = jnp.where((c == 0) == first, y, value)
        return dev(zz, yy * 2 + c, x)

    mate = dev(z, y * 2 + 1 - c, x)

    @pl.loop(1, 8)
    def _(j):
        block = jx.at[c, outer, inner]
        remote(block, block, s_ph.at[10], r_ph.at[10], along(lax.rem(inner + j, 8), True)).start()

    pltpu.make_async_copy(jx.at[0, 0, pl.ds(0, 7)], jx.at[0, 0, pl.ds(0, 7)], r_ph.at[10]).wait()

    def j_copy(j):
        block = jx.at[c, outer]
        return remote(block, block, s_ph.at[11], r_j.at[outer], along(lax.rem(outer + j, 8), False))

    def m_forward(at):
        block = jx.at[c, at]
        return remote(block, block, s_ph.at[12], r_ph.at[12], mate)

    @pl.loop(1, 8)
    def _(j):
        j_copy(j).start()

    m_forward(outer).start()

    into = (iota((256, 128), 0) >> 1 == iota((256, 128), 1)).astype(bf16)
    group_of = dot_t(into, jnp.broadcast_to(source, (8, 128)).astype(bf16))[:, 0:1]
    request_id = iota((256, 256), 0)
    spot = iota((256, 256), 1)
    held_row = ((spot >> 3) & 7) * 32 + (spot >> 7) * 16 + ((spot >> 6) & 1) * 8 + (spot & 7)
    wanted = jnp.where((request_id & 1) == 0, request_id.astype(f32), 2.0 * group_of + 1.0)
    back = (held_row.astype(f32) == wanted).astype(bf16)

    @pl.loop(1, 8)
    def _(j):
        at = lax.rem(outer + 8 - j, 8)
        block = jx.at[c, at]
        remote(block, block, s_ph.at[11], r_j.at[at], mate).wait_recv()
        m_forward(at).start()

    pltpu.make_async_copy(jx.at[0], jx.at[0], r_ph.at[12]).wait()
    for a in range(4):
        blocks = []
        for h in range(2):
            blocks.append(jx[0, 2 * a + h].reshape(64, 128))
            blocks.append(jx[1, :, 2 * a + h].reshape(64, 128))
        out_ref[:, a * 128:(a + 1) * 128] = dot(back, jnp.concatenate(blocks, axis=0)).astype(bf16)

    stores[2].start()


    def sent(block, sem):
        pltpu.make_async_copy(block, block, sem).wait()

    for m in range(2):
        for a in range(4):
            src, dst, which = w1_parts(a)[m]
            target = a * 4 + cls

            @pl.when(target != yc)
            def _():
                remote(src, dst, s_w1.at[which, a], r_w1.at[which], dev(z, target, x)).wait_send()

    sent(seven(win_w), s_z.at[0])
    sent(seven(wo_w), s_z.at[1])
    for step in range(1, 5):
        for which in range(2):
            for way in ways(step):
                ring(step, way, which).wait_send()
    sent(hx.at[three], s_ph.at[0])
    sent(rb.at[fifteen], s_ph.at[1])
    sent(cx.at[three], s_ph.at[2])
    sent(dx.at[three], s_ph.at[3])
    sent(ex.at[fifteen], s_ph.at[4])
    sent(ox.at[three], s_ph.at[5])
    sent(mx.at[fifteen], s_ph.at[6])
    sent(gu_w.at[z, pl.ds(0, 15)], s_ph.at[7])
    sent(ax.at[fifteen], s_ph.at[8])
    sent(yx.at[three], s_ph.at[9])
    sent(jx.at[0, 0, pl.ds(0, 7)], s_ph.at[10])
    sent(jx.at[0, pl.ds(0, 7)], s_ph.at[11])
    sent(jx.at[0], s_ph.at[12])
    for store in stores:
        store.wait()


def hand_over(a_ref, b_ref, c_ref, a_out, b_out, c_out, a_buf, b_buf, c_buf, sem_in, sem_out):
    parts = [(a_ref.at[k], a_buf.at[k], a_out.at[k]) for k in range(4)]
    parts = [(c_ref, c_buf, c_out)] + parts + [(b_ref, b_buf, b_out)]
    ins = [pltpu.make_async_copy(src, buf, sem_in.at[k]) for k, (src, buf, _) in enumerate(parts)]
    outs = [pltpu.make_async_copy(buf, dst, sem_out.at[k]) for k, (_, buf, dst) in enumerate(parts)]
    for copy in ins:
        copy.start()
    for arrived, leaves in zip(ins, outs):
        arrived.wait()
        leaves.start()
    for copy in outs:
        copy.wait()


def rotation_table():
    half = HD // 2
    frequency = np.float32(10000.0) ** (-np.arange(half, dtype=np.float32) / np.float32(half))
    positions = (PAGE * np.arange(1, NP + 1)).astype(np.float32)
    angles = np.tile((positions[:, None] * frequency[None, :]).astype(np.float64), (1, 4))
    return np.concatenate([np.cos(angles), np.sin(angles)], axis=0).astype(np.float32)


def on_device(
    hidden_in, attention_gain, query_gain, key_gain, feedforward_gain,
    input_weight, output_weight, gate_weight, up_weight, down_weight,
    old_cache, keep_rows, drop_weights, dest_slots, lengths, page_table, source,
):
    operands = (
        hidden_in, input_weight, output_weight, gate_weight, up_weight, down_weight,
        old_cache, keep_rows, drop_weights, dest_slots,
        lengths[None, :], page_table, source[None, :],
        attention_gain[None, :], feedforward_gain[None, :], query_gain[None, :], key_gain[None, :],
        jnp.asarray(rotation_table()),
    )
    hbm = pl.BlockSpec(memory_space=pltpu.HBM)
    dma = pltpu.SemaphoreType.DMA

    def scratch(*shape, dtype=f32):
        return pltpu.VMEM(shape, dtype)

    results = pl.pallas_call(
        kernel,
        name="decode",
        out_shape=(
            jax.ShapeDtypeStruct((4, PAGE, KVW), bf16),
            jax.ShapeDtypeStruct((8, KVW), bf16),
            jax.ShapeDtypeStruct(hidden_in.shape, bf16),
        ),
        in_specs=[hbm] * len(operands),
        out_specs=(hbm, hbm, hbm),
        scratch_shapes=[
            (pltpu.SMEM if k == 9 else pltpu.VMEM)(a.shape, a.dtype) for k, a in enumerate(operands)
        ] + [
            scratch(4, 32, 512, dtype=bf16),
            scratch(4, 16, 128, dtype=bf16),
            scratch(16, 16, 256, dtype=bf16),
            scratch(4, 3, 16, 128, dtype=bf16),
            scratch(8, 16, 512, dtype=bf16),
            scratch(8, 4, 16, 128, dtype=bf16),
            scratch(8, 16, 16, 256, dtype=bf16),
            scratch(8, 2, 8, 16, 128, dtype=bf16),
            scratch(16, 2, 512),
            scratch(16, 2, 512),
            scratch(4, 4, 2, 128),
            scratch(32, 128),
            scratch(10, 64, 640, dtype=bf16),
            scratch(16, 640),
            scratch(4, 2 * QROWS, 128),
            scratch(4, 2, 512),
            scratch(16, 2, 512),
            scratch(32, 512),
            scratch(4, 32, 128),
            scratch(16, 32, 128, dtype=bf16),
            scratch(32, 128),
            scratch(16, 32, 128, dtype=bf16),
            scratch(4, 8, 128),
            scratch(4, 8, 128),
            scratch(2, 8, 8, 8, 128, dtype=bf16),
            scratch(8, 640),
            scratch(8, 1, 640),
            scratch(4, PAGE, KVW, dtype=bf16),
            scratch(8, KVW, dtype=bf16),
            scratch(*hidden_in.shape, dtype=bf16),
            dma((len(operands),)), dma((3,)),
            dma((2, 4)), dma((2,)),
            dma((2,)), dma((2,)),
            dma((2, 4, 2)), dma((2, 4, 2)),
            dma((13,)), dma((13,)), dma((8,)),
        ],
        compiler_params=pltpu.CompilerParams(
            collective_id=0, has_side_effects=True, vmem_limit_bytes=63 << 20
        ),
    )(*operands)
    return pl.pallas_call(
        hand_over,
        name="hand_over",
        out_shape=tuple(jax.ShapeDtypeStruct(a.shape, a.dtype) for a in results),
        in_specs=[hbm] * 3,
        out_specs=(hbm,) * 3,
        scratch_shapes=[pltpu.VMEM(a.shape, a.dtype) for a in results] + [dma((6,)), dma((6,))],
    )(*results)


def solution(mesh):
    placed = (
        P(None, "head"),
        P(),
        P(),
        P(),
        P(),
        P("req", "head"),
        P("req", "head"),
        P("req", "head"),
        P("req", "head"),
        P("req", "head"),
        P(("req", "head"), None, None),
        P(("req", "head"), None),
        P(("req", "head"), None),
        P(("req", "head"), None),
        P(),
        P("req", None),
        P(),
    )
    return jax.shard_map(
        on_device,
        mesh=mesh,
        in_specs=placed,
        out_specs=(P(("req", "head"), None, None), P(("req", "head"), None), P(None, "head")),
        check_vma=False,
    )
```
